128 devices in a mesh: rhs: 4 (over y), rows: 32 (over x, z, core).
Axes of the slice: x: 4, y: 4, z: 4, core: 2. Of those that a mesh axis runs over, the one named last changes fastest.
Arguments:
- right_side: float32 [65536, 512], P('rows', 'rhs'), may hold values from -6 to 6
- fine_blocks: bfloat16 [512, 32, 128, 128], P('rows'), may hold values from -0.09375 to 0.09375
- fine_columns: int32 [512, 32], P('rows'), may hold values from 0 to 511, as said below
- fine_diag: float32 [65536], P('rows'), may hold values from 3 to 6
- aggregate: int32 [512], P('rows'), may hold values from 0 to 127, as said below
- coarse_blocks: float32 [128, 3, 128, 128], P(('rhs', 'rows')), may hold values from -0.3125 to 0.3125
- coarse_diag: float32 [16384], P(('rhs', 'rows')), may hold values from 1 to 2
Outputs:
- solution: float32 [65536, 512], P('rows', 'rhs')
The draws below stay inside these ranges and needn't reach their ends.
Inputs may be any that keep to these rules, and one draw needn't show every extreme that they name: `fine_columns`: the 32 stored blocks of fine block-row r have 32 distinct columns, each equal to r + o modulo 512 for an offset o from -16 to 16, and every row holds both end offsets. `aggregate`: fine block-row r maps to a coarse block c with c % (32) equal to r // 16; every coarse block receives one or more fine block-rows.
All inputs are finite; a program needn't handle non-finite values.
Results may differ from the reference program's by a relative error of at most 0.004.
Values may be sent and summed in bfloat16 or wider, within the bound.
No kernel may reach another device: no remote copies, remote signals or barrier semaphores. Data moves between devices by JAX's collectives and lax.ppermute only.
A program may use at most 128 MiB of HBM per device.

```python
import jax
import jax.numpy as jnp
from jax import lax

B = 128
K = 32
BR_DEV = 16
CYCLES = 2
SWEEPS = 2
CHEB = 3
NB = 512
NF = 65536
NCB = 128
RHS = 512


def shuffle_band(row_key):
    return jax.random.permutation(row_key, K)


def draw_fine_columns(key, part):
    reach = K // 2
    block_ids = jnp.arange(NB, dtype=jnp.int32)[:, None]
    dropped = jax.random.randint(key, (NB, 1), 1 - reach, reach, dtype=jnp.int32)
    base = jnp.arange(K, dtype=jnp.int32)[None, :] - reach
    offsets = base + (base >= dropped).astype(jnp.int32)
    row_keys = jax.random.split(jax.random.fold_in(key, 3), NB)
    orders = jax.vmap(shuffle_band)(row_keys)
    offsets = jnp.take_along_axis(offsets, orders, axis=1)
    return jnp.mod(block_ids + offsets, NB).astype(jnp.int32)


def shuffle_row(row_key):
    return jax.random.permutation(row_key, BR_DEV)


def draw_aggregate(key, part):
    device_rows = NB // BR_DEV
    groups = NCB // device_rows
    group_ids = jax.random.randint(key, (device_rows, BR_DEV), 0, groups, dtype=jnp.int32)
    group_ids = group_ids.at[:, :groups].set(jnp.arange(groups, dtype=jnp.int32)[None, :])
    row_keys = jax.random.split(jax.random.fold_in(key, 7), device_rows)
    orders = jax.vmap(shuffle_row)(row_keys)
    group_ids = jnp.take_along_axis(group_ids, orders, axis=1)
    owners = jnp.arange(device_rows, dtype=jnp.int32)[:, None]
    return (group_ids * device_rows + owners).reshape(NB).astype(jnp.int32)


def level_of(rng, dims, shards, least, largest):
    def one(dim, shards_of):
        steps = jax.random.uniform(jax.random.fold_in(jax.random.fold_in(rng, 6), dim), (shards_of,), jnp.float32, least / len(shards), largest / len(shards))
        return jnp.repeat(jnp.exp(steps), dims[dim] // shards_of).reshape((-1,) + (1,) * (len(dims) - dim - 1))

    gain = one(*shards[0])
    for cut in shards[1:]:
        gain = gain * one(*cut)
    return gain


def bell_draw(key, extent, scale, bound, shards=(), kind=jnp.bfloat16):
    entries = jax.random.normal(key, extent, jnp.float32) * scale
    if len(shards) > 0:
        entries = level_of(key, extent, shards, -0.22, 0.18) * entries
    return jnp.clip(entries, min=-bound, max=bound).astype(kind)


def setup_inputs(seed: int = 0) -> dict:
    arg_keys = jax.random.split(jax.random.key(seed), 8)
    right_side = bell_draw(arg_keys[0], (NF, RHS), 1.0, 6.0, ((0, 32), (1, 4)), jnp.float32)
    fine_blocks = bell_draw(arg_keys[1], (NB, K, B, B), (K * B) ** -0.5, 0.09375, ((0, 32),))
    fine_columns = draw_fine_columns(jax.random.fold_in(arg_keys[7], 71), 0)
    fine_diag = jnp.clip(3.0 + 3.0 * jax.random.uniform(arg_keys[3], (NF,), jnp.float32) ** level_of(arg_keys[3], (NF,), ((0, 32),), -0.2, 0.2), 3.0, 6.0)
    aggregate = draw_aggregate(jax.random.fold_in(arg_keys[7], 71), 0)
    coarse_blocks = bell_draw(arg_keys[5], (NCB, 3, B, B), (3 * B) ** -0.5, 0.3125, ((0, 128),), jnp.float32)
    coarse_diag = jnp.clip(1.0 + 1.0 * jax.random.uniform(arg_keys[6], (NCB * B,), jnp.float32) ** level_of(arg_keys[6], (NCB * B,), ((0, 128),), -0.2, 0.2), 1.0, 2.0)
    return dict(right_side=right_side, fine_blocks=fine_blocks, fine_columns=fine_columns, fine_diag=fine_diag, aggregate=aggregate, coarse_blocks=coarse_blocks, coarse_diag=coarse_diag)


relax_weight = 0.7
centre = 1.0
half_width = 0.6


def fine_apply(field, fine_blocks, fine_columns, fine_scale):
    rounded = field.astype(jnp.bfloat16)

    def one_row(pair):
        row_blocks, row_columns = pair
        picked = rounded[row_columns].astype(jnp.float32)
        return jnp.einsum("kij,kjn->in", row_blocks.astype(jnp.float32), picked)

    product = lax.map(one_row, (fine_blocks, fine_columns))
    return fine_scale * field + product


def coarse_apply(field, coarse_blocks, coarse_scale):
    empty = jnp.zeros((1,) + field.shape[1:], jnp.float32)
    lower_rim = jnp.concatenate([empty, field[:-1]], axis=0)
    upper_rim = jnp.concatenate([field[1:], empty], axis=0)
    high = lax.Precision.HIGHEST
    total = coarse_scale * field
    total = total + jnp.einsum("cij,cjn->cin", coarse_blocks[:, 0], lower_rim, precision=high)
    total = total + jnp.einsum("cij,cjn->cin", coarse_blocks[:, 1], field, precision=high)
    total = total + jnp.einsum("cij,cjn->cin", coarse_blocks[:, 2], upper_rim, precision=high)
    return total


def chebyshev(source, coarse_blocks, coarse_scale):
    sigma_ratio = centre / half_width
    ratio_old = 1.0 / sigma_ratio
    update = source / coarse_scale / centre
    correction = update
    for step_index in range(CHEB - 1):
        ratio_new = 1.0 / (2.0 * sigma_ratio - ratio_old)
        scaled = (source - coarse_apply(correction, coarse_blocks, coarse_scale)) / coarse_scale
        update = ratio_new * ratio_old * update + (2.0 * ratio_new / half_width) * scaled
        correction = correction + update
        ratio_old = ratio_new
    return correction


def reference(right_side, fine_blocks, fine_columns, fine_diag, aggregate, coarse_blocks, coarse_diag):
    source = right_side.reshape(NB, B, RHS)
    fine_scale = fine_diag.reshape(NB, B, 1)
    coarse_scale = coarse_diag.reshape(NCB, B, 1)
    solution = jnp.zeros((NB, B, RHS), jnp.float32)
    for turn_index in range(CYCLES):
        for sweep_index in range(SWEEPS):
            if turn_index == 0 and sweep_index == 0:
                solution = relax_weight * source / fine_scale
            else:
                solution = solution + relax_weight * (source - fine_apply(solution, fine_blocks, fine_columns, fine_scale)) / fine_scale
        residual = source - fine_apply(solution, fine_blocks, fine_columns, fine_scale)
        coarse_side = jax.ops.segment_sum(residual, aggregate, num_segments=NCB)
        correction = chebyshev(coarse_side, coarse_blocks, coarse_scale)
        solution = solution + correction[aggregate]
        for sweep_index in range(SWEEPS):
            solution = solution + relax_weight * (source - fine_apply(solution, fine_blocks, fine_columns, fine_scale)) / fine_scale
    return solution.reshape(NF, RHS)
```

```python
import jax
import jax.numpy as jnp
from jax import lax
from jax.experimental import pallas as pl
from jax.experimental.pallas import tpu as pltpu
from jax.sharding import PartitionSpec as P

CYCLES = 2
CHEB = 3
RELAX = 0.7
THETA = 1.0
DELTA = 0.6

B = 128
ROWS = 16
GROUP = 4
TILE = GROUP * B
TILE_ROWS = ROWS // GROUP
SLOTS = 36
FIELD = ROWS * B
TAIL = 16
QROWS = 4 * B

f32 = jnp.float32
bf16 = jnp.bfloat16
VMEM_SPEC = pl.BlockSpec(memory_space=pltpu.VMEM)
SMEM_SPEC = pl.BlockSpec(memory_space=pltpu.SMEM)
ANY_SPEC = pl.BlockSpec(memory_space=pl.ANY)
LIMIT = 12 * 1024 * 1024


def resident(x):
    return pltpu.with_memory_space_constraint(x, pltpu.VMEM)


def core_of():
    return lax.rem(lax.axis_index("rows"), 2)


def column(row):
    return jnp.transpose(jnp.broadcast_to(row, (B, B)))


def start_kernel(right_ref, diag_ref, group_ref, first_ref, sent_ref, ratio_ref, diag_out_ref):
    for r in range(ROWS):
        rows = pl.ds(r * B, B)
        diag = column(diag_ref[r : r + 1, :])
        ratio = RELAX / diag
        value = ratio * right_ref[rows, :]
        diag_out_ref[rows, :] = diag
        ratio_ref[rows, :] = ratio
        first_ref[rows, :] = value
        sent_ref[rows, :] = value.astype(bf16)
    index = lax.broadcasted_iota(jnp.int32, (TAIL, B), 0)
    tail = jnp.zeros((TAIL, B), f32)
    for r in range(ROWS):
        tail = jnp.where(index == r, group_ref[r].astype(f32), tail)
    sent_ref[pl.ds(FIELD, TAIL), :] = tail.astype(bf16)


def load_kernel(columns_ref, blocks_ref, kept_ref, sem):
    first = lax.axis_index("rows") * ROWS - ROWS
    empty = jnp.zeros((B, B), bf16)

    @pl.loop(0, ROWS)
    def _(r):
        lead = lax.rem(r, GROUP)
        base = r * SLOTS
        total = jnp.int32(0)
        for k in range(2 * ROWS):
            offset = jnp.bitwise_and(columns_ref[r, k] - first - r + 512, 511)
            offset = jnp.minimum(offset, 2 * ROWS)
            pltpu.make_async_copy(blocks_ref.at[r, k], kept_ref.at[base + lead + offset], sem).start()
            total = total + offset
        missing = jnp.clip(ROWS * (2 * ROWS + 1) - total, 0, 2 * ROWS)
        kept_ref[base + lead + missing] = empty
        for pad in range(GROUP - 1):
            place = jnp.where(pad < lead, pad, 2 * ROWS + 1 + pad)
            kept_ref[base + place] = empty

    @pl.loop(0, ROWS)
    def _(r):
        pltpu.make_async_copy(
            blocks_ref.at[r], kept_ref.at[pl.ds(r * 2 * ROWS, 2 * ROWS)], sem
        ).wait()


def pack_kernel(blocks_ref, diag_ref, out_ref):
    inverse = 1.0 / diag_ref[...]
    scale = column(inverse)
    for d in range(3):
        out_ref[pl.ds(d * B, B), :] = (scale * blocks_ref[0, d]).astype(bf16)
    high = inverse.astype(bf16).astype(f32)
    low = inverse - high
    index = lax.broadcasted_iota(jnp.int32, (TAIL, B), 0)
    out_ref[pl.ds(3 * B, TAIL), :] = jnp.where(index == 0, high, low).astype(bf16)


def sort_kernel(p0_ref, p1_ref, p2_ref, p3_ref, ops_ref, scale_ref):
    me = lax.axis_index("rhs")
    for k, ref in enumerate((p0_ref, p1_ref, p2_ref, p3_ref)):
        q = jnp.bitwise_and(me - k + 4, 3)
        for d in range(3):
            ops_ref[q * 3 + d] = ref[pl.ds(d * B, B), :]
        tail = ref[pl.ds(3 * B, TAIL), :].astype(f32)
        scale_ref[pl.ds(q * B, B), :] = column(tail[0:1, :] + tail[1:2, :])


def tile_product(kept_ref, group, slot, count, field):
    lhs = jnp.concatenate(
        [
            jnp.concatenate(
                [kept_ref[(group * GROUP + a) * SLOTS + slot + b] for b in range(GROUP * count)],
                axis=1,
            )
            for a in range(GROUP)
        ],
        axis=0,
    )
    return jnp.dot(lhs, field, preferred_element_type=f32)


def side_product(kept_ref, upper, m, field_ref):
    group = jnp.where(upper, m, TILE_ROWS - 1 - m)
    start = pl.multiple_of(jnp.where(upper, 0, TILE * (TILE_ROWS - 1 - m)), TILE)
    slot = jnp.where(upper, GROUP * (2 * TILE_ROWS - m), 0)
    field = field_ref[pl.ds(start, TILE * (m + 1)), :]
    return group, tile_product(kept_ref, group, slot, m + 1, field)


def near_products(kept_ref, own_ref, near_ref, emit):
    upper = core_of() == 0
    own = own_ref[pl.ds(0, FIELD), :]
    for m in range(TILE_ROWS):
        group, part = side_product(kept_ref, upper, m, near_ref)
        slot = GROUP * (TILE_ROWS - group)
        part = part + tile_product(kept_ref, group, slot, TILE_ROWS, own)
        emit(pl.ds(pl.multiple_of(group * TILE, TILE), TILE), part)


def far_products(kept_ref, far_ref, emit):
    upper = core_of() == 1
    for m in range(TILE_ROWS):
        group, part = side_product(kept_ref, upper, m, far_ref)
        emit(pl.ds(pl.multiple_of(group * TILE, TILE), TILE), part)


def sweep_near_kernel(kept_ref, own_ref, near_ref, x_ref, first_ref, ratio_ref, base_ref):
    def emit(rows, part):
        base_ref[rows, :] = (1.0 - RELAX) * x_ref[rows, :] + first_ref[rows, :] - ratio_ref[rows, :] * part

    near_products(kept_ref, own_ref, near_ref, emit)


def sweep_far_kernel(kept_ref, far_ref, base_ref, ratio_ref, x_ref, sent_ref):
    def emit(rows, part):
        value = base_ref[rows, :] - ratio_ref[rows, :] * part
        x_ref[rows, :] = value
        sent_ref[rows, :] = value.astype(bf16)

    far_products(kept_ref, far_ref, emit)


def last_far_kernel(kept_ref, far_ref, base_ref, ratio_ref, x_ref):
    def emit(rows, part):
        x_ref[rows, :] = base_ref[rows, :] - ratio_ref[rows, :] * part

    far_products(kept_ref, far_ref, emit)


def residual_near_kernel(kept_ref, own_ref, near_ref, x_ref, right_ref, diag_ref, base_ref):
    def emit(rows, part):
        base_ref[rows, :] = right_ref[rows, :] - diag_ref[rows, :] * x_ref[rows, :] - part

    near_products(kept_ref, own_ref, near_ref, emit)


def residual_far_kernel(kept_ref, group_ref, far_ref, base_ref, scale_ref, res_ref, side_ref, sent_ref):
    def emit(rows, part):
        res_ref[rows, :] = base_ref[rows, :] - part

    far_products(kept_ref, far_ref, emit)
    side_ref[...] = jnp.zeros((QROWS, B), f32)
    for r in range(ROWS):
        rows = pl.ds(pl.multiple_of(group_ref[r] * B, B), B)
        side_ref[rows, :] += res_ref[pl.ds(r * B, B), :]
    value = scale_ref[...] * side_ref[...]
    side_ref[...] = value
    sent_ref[...] = value.astype(bf16)


def spread(coarse_ref, tail_ref, out_ref):
    tail = tail_ref[pl.ds(FIELD, TAIL), :].astype(f32)
    parts = [coarse_ref[pl.ds(q * B, B), :].astype(f32) for q in range(4)]
    for r in range(ROWS):
        group = tail[r : r + 1, :]
        value = jnp.where(group < 0.5, parts[0], parts[1])
        value = jnp.where(group < 1.5, value, parts[2])
        value = jnp.where(group < 2.5, value, parts[3])
        out_ref[pl.ds(r * B, B), :] = value.astype(bf16)


def lift_near_kernel(
    kept_ref, group_ref, coarse_ref, near_ref, near_tail_ref, x_ref, res_ref, ratio_ref, base_ref, own_s, near_s
):
    for r in range(ROWS):
        rows = pl.ds(pl.multiple_of(group_ref[r] * B, B), B)
        own_s[pl.ds(r * B, B), :] = coarse_ref[rows, :]
    spread(near_ref, near_tail_ref, near_s)

    def emit(rows, part):
        base_ref[rows, :] = (
            x_ref[rows, :]
            + (1.0 - RELAX) * own_s[rows, :].astype(f32)
            + ratio_ref[rows, :] * (res_ref[rows, :] - part)
        )

    near_products(kept_ref, own_s, near_s, emit)


def lift_far_kernel(kept_ref, far_ref, far_tail_ref, base_ref, ratio_ref, x_ref, sent_ref, far_s):
    spread(far_ref, far_tail_ref, far_s)
    sweep_far_kernel(kept_ref, far_s, base_ref, ratio_ref, x_ref, sent_ref)


def coarse_terms(ops_ref, own_ref, near_ref, far_ref, emit):
    i = lax.axis_index("rows")
    last = lax.axis_size("rows") - 1
    near_is_upper = (core_of() == 0).astype(f32)
    step_up = (i == last).astype(jnp.int32)
    step_down = (i == 0).astype(jnp.int32)
    for q in range(4):
        at_up = pl.multiple_of(jnp.minimum(q + step_up, 3) * B, B)
        at_down = pl.multiple_of(jnp.maximum(q - step_down, 0) * B, B)
        keep_up = (q + step_up <= 3).astype(f32)
        keep_down = (q - step_down >= 0).astype(f32)
        upper = near_is_upper * near_ref[pl.ds(at_up, B), :].astype(f32) + (
            1.0 - near_is_upper
        ) * far_ref[pl.ds(at_up, B), :].astype(f32)
        lower = near_is_upper * far_ref[pl.ds(at_down, B), :].astype(f32) + (
            1.0 - near_is_upper
        ) * near_ref[pl.ds(at_down, B), :].astype(f32)
        field = jnp.concatenate(
            [
                (keep_down * lower).astype(bf16),
                own_ref[pl.ds(q * B, B), :],
                (keep_up * upper).astype(bf16),
            ],
            axis=0,
        )
        ops = jnp.concatenate([ops_ref[q * 3 + d] for d in range(3)], axis=1)
        emit(pl.ds(q * B, B), jnp.dot(ops, field, preferred_element_type=f32))


def ratios():
    sigma = THETA / DELTA
    old = 1.0 / sigma
    out = []
    for _ in range(CHEB - 1):
        new = 1.0 / (2.0 * sigma - old)
        out.append((new * old, 2.0 * new / DELTA))
        old = new
    return out


def coarse_first_kernel(ops_ref, side_ref, own_ref, near_ref, far_ref, fix_ref, sent_ref):
    keep, gain = ratios()[0]

    def emit(rows, part):
        side = side_ref[rows, :] / THETA
        fix = side + keep * side + gain * (side_ref[rows, :] - side - part)
        fix_ref[rows, :] = fix
        sent_ref[rows, :] = fix.astype(bf16)

    coarse_terms(ops_ref, own_ref, near_ref, far_ref, emit)


def coarse_second_kernel(ops_ref, side_ref, fix_ref, own_ref, near_ref, far_ref, sent_ref):
    keep, gain = ratios()[1]

    def emit(rows, part):
        fix = fix_ref[rows, :]
        update = fix - side_ref[rows, :] / THETA
        fix = fix + keep * update + gain * (side_ref[rows, :] - fix - part)
        sent_ref[rows, :] = fix.astype(bf16)

    coarse_terms(ops_ref, own_ref, near_ref, far_ref, emit)


def run(kernel, outs, args, scratch=(), cost=(0, 0), limit=None):
    specs, values = [], []
    for value, space in args:
        if space == "v":
            specs.append(VMEM_SPEC)
            values.append(resident(value))
        elif space == "b":
            specs.append(VMEM_SPEC)
            values.append(value)
        elif space == "s":
            specs.append(SMEM_SPEC)
            values.append(value)
        else:
            specs.append(ANY_SPEC)
            values.append(value)
    return pl.pallas_call(
        kernel,
        out_shape=[pltpu.VMEM(shape, dtype) for shape, dtype in outs],
        in_specs=specs,
        out_specs=[VMEM_SPEC] * len(outs),
        scratch_shapes=list(scratch),
        cost_estimate=pl.CostEstimate(flops=cost[0], bytes_accessed=cost[1], transcendentals=0),
        compiler_params=pltpu.CompilerParams(vmem_limit_bytes=limit or LIMIT),
    )(*values)


def swap(x, size):
    far = lax.ppermute(
        x, "rows", [(i, (i - 1) % size if i % 2 == 0 else (i + 1) % size) for i in range(size)]
    )
    near = lax.ppermute(x, "rows", [(i, i ^ 1) for i in range(size)])
    return near, far


FULL = (FIELD, B)
SIDE = (QROWS, B)
NEAR_COST = (2 * 26 * TILE * TILE * B, 8_000_000)
FAR_COST = (2 * 10 * TILE * TILE * B, 3_000_000)


def shards(right_side, fine_blocks, fine_columns, fine_diag, aggregate, coarse_blocks, coarse_diag):
    size = lax.axis_size("rows")
    group = aggregate // size
    diag_rows = fine_diag.reshape(ROWS, B)

    first, sent, ratio, diag = run(
        start_kernel,
        [(FULL, f32), ((FIELD + TAIL, B), bf16), (FULL, f32), (FULL, f32)],
        [(right_side, "b"), (diag_rows, "b"), (group, "s")],
    )
    near, far = swap(sent, size)
    near_tail, far_tail = near, far
    (kept,) = run(
        load_kernel,
        [((ROWS * SLOTS, B, B), bf16)],
        [(fine_columns, "s"), (fine_blocks, "a")],
        [pltpu.SemaphoreType.DMA],
        (0, 20_000_000),
    )
    (packed,) = run(
        pack_kernel,
        [((3 * B + TAIL, B), bf16)],
        [(coarse_blocks, "b"), (coarse_diag.reshape(1, B), "b")],
    )
    pieces = [packed] + [
        lax.ppermute(packed, "rhs", [(i, (i + k) % 4) for i in range(4)]) for k in range(1, 4)
    ]
    ops, scale = run(
        sort_kernel, [((12, B, B), bf16), (SIDE, f32)], [(p, "v") for p in pieces]
    )

    def sweep(x, sent, near, far, last=False):
        (base,) = run(
            sweep_near_kernel,
            [(FULL, f32)],
            [(kept, "v"), (sent, "v"), (near, "v"), (x, "v"), (first, "v"), (ratio, "v")],
            cost=NEAR_COST,
        )
        args = [(kept, "v"), (far, "v"), (base, "v"), (ratio, "v")]
        if last:
            return run(last_far_kernel, [(FULL, f32)], args, cost=FAR_COST)
        return run(sweep_far_kernel, [(FULL, f32), (FULL, bf16)], args, cost=FAR_COST)

    x = first
    for turn in range(CYCLES):
        if turn > 0:
            near, far = swap(sent, size)
            x, sent = sweep(x, sent, near, far)
            near, far = swap(sent, size)
        x, sent = sweep(x, sent, near, far)
        near, far = swap(sent, size)
        (base,) = run(
            residual_near_kernel,
            [(FULL, f32)],
            [(kept, "v"), (sent, "v"), (near, "v"), (x, "v"), (right_side, "b"), (diag, "v")],
            cost=NEAR_COST,
        )
        res, side, sent = run(
            residual_far_kernel,
            [(FULL, f32), (SIDE, f32), (SIDE, bf16)],
            [(kept, "v"), (group, "s"), (far, "v"), (base, "v"), (scale, "v")],
            cost=FAR_COST,
        )
        near, far = swap(sent, size)
        fix, sent = run(
            coarse_first_kernel,
            [(SIDE, f32), (SIDE, bf16)],
            [(ops, "v"), (side, "v"), (sent, "v"), (near, "v"), (far, "v")],
        )
        near, far = swap(sent, size)
        (sent,) = run(
            coarse_second_kernel,
            [(SIDE, bf16)],
            [(ops, "v"), (side, "v"), (fix, "v"), (sent, "v"), (near, "v"), (far, "v")],
        )
        near, far = swap(sent, size)
        (base,) = run(
            lift_near_kernel,
            [(FULL, f32)],
            [
                (kept, "v"), (group, "s"), (sent, "v"), (near, "v"), (near_tail, "v"),
                (x, "v"), (res, "v"), (ratio, "v"),
            ],
            [pltpu.VMEM(FULL, bf16), pltpu.VMEM(FULL, bf16)],
            NEAR_COST,
        )
        x, sent = run(
            lift_far_kernel,
            [(FULL, f32), (FULL, bf16)],
            [(kept, "v"), (far, "v"), (far_tail, "v"), (base, "v"), (ratio, "v")],
            [pltpu.VMEM(FULL, bf16)],
            FAR_COST,
        )
        near, far = swap(sent, size)
        if turn < CYCLES - 1:
            x, sent = sweep(x, sent, near, far)
        else:
            (x,) = sweep(x, sent, near, far, last=True)
    return x


def solution(mesh):
    in_specs = (
        P("rows", "rhs"),
        P("rows", None, None, None),
        P("rows", None),
        P("rows"),
        P("rows"),
        P(("rhs", "rows"), None, None, None),
        P(("rhs", "rows")),
    )
    return jax.shard_map(
        shards, mesh=mesh, in_specs=in_specs, out_specs=P("rows", "rhs"), check_vma=False
    )
```

```python
import jax
import jax.numpy as jnp
from jax import lax
from jax.experimental import pallas as pl
from jax.experimental.pallas import tpu as pltpu
from jax.sharding import PartitionSpec as P

CYCLES = 2
CHEB = 3
RELAX = 0.7
THETA = 1.0
DELTA = 0.6

B = 128
ROWS = 16
GROUP = 4
TILE = GROUP * B
TILE_ROWS = ROWS // GROUP
SLOTS = 36
FIELD = ROWS * B
TAIL = 16
QROWS = 4 * B

f32 = jnp.float32
bf16 = jnp.bfloat16
VMEM_SPEC = pl.BlockSpec(memory_space=pltpu.VMEM)
SMEM_SPEC = pl.BlockSpec(memory_space=pltpu.SMEM)
ANY_SPEC = pl.BlockSpec(memory_space=pl.ANY)
LIMIT = 12 * 1024 * 1024


def resident(x):
    return pltpu.with_memory_space_constraint(x, pltpu.VMEM)


def core_of():
    return lax.rem(lax.axis_index("rows"), 2)


def column(row):
    return jnp.transpose(jnp.broadcast_to(row, (B, B)))


def start_kernel(
    right_ref, diag_ref, group_ref, first_ref, sent_ref, ratio_ref, diag_out_ref, right_s, diag_s, group_s, sems
):
    chunks = [
        pltpu.make_async_copy(
            right_ref.at[pl.ds(g * TILE, TILE), :], right_s.at[pl.ds(g * TILE, TILE), :], sems.at[g]
        )
        for g in range(TILE_ROWS)
    ]
    diag_copy = pltpu.make_async_copy(diag_ref, diag_s, sems.at[TILE_ROWS])
    group_copy = pltpu.make_async_copy(group_ref, group_s, sems.at[TILE_ROWS + 1])
    diag_copy.start()
    for chunk in chunks:
        chunk.start()
    group_copy.start()
    diag_copy.wait()
    for g in range(TILE_ROWS):
        chunks[g].wait()
        for r in range(g * GROUP, (g + 1) * GROUP):
            rows = pl.ds(r * B, B)
            diag = column(diag_s[r : r + 1, :])
            ratio = RELAX / diag
            value = ratio * right_s[rows, :]
            diag_out_ref[rows, :] = diag
            ratio_ref[rows, :] = ratio
            first_ref[rows, :] = value
            sent_ref[rows, :] = value.astype(bf16)
    group_copy.wait()
    size = lax.axis_size("rows")
    index = lax.broadcasted_iota(jnp.int32, (TAIL, B), 0)
    tail = jnp.zeros((TAIL, B), f32)
    for r in range(ROWS):
        tail = jnp.where(index == r, lax.div(group_s[r], size).astype(f32), tail)
    sent_ref[pl.ds(FIELD, TAIL), :] = tail.astype(bf16)


def pack_kernel(blocks_ref, diag_ref, out_ref):
    inverse = 1.0 / diag_ref[...]
    scale = column(inverse)
    for d in range(3):
        out_ref[pl.ds(d * B, B), :] = (scale * blocks_ref[0, d]).astype(bf16)
    high = inverse.astype(bf16).astype(f32)
    low = inverse - high
    index = lax.broadcasted_iota(jnp.int32, (TAIL, B), 0)
    out_ref[pl.ds(3 * B, TAIL), :] = jnp.where(index == 0, high, low).astype(bf16)


def sort_kernel(p0_ref, p1_ref, p2_ref, p3_ref, after_ref, ops_ref, scale_ref):
    me = lax.axis_index("rhs")
    for k, ref in enumerate((p0_ref, p1_ref, p2_ref, p3_ref)):
        q = jnp.bitwise_and(me - k + 4, 3)
        for d in range(3):
            ops_ref[q * 3 + d] = ref[pl.ds(d * B, B), :]
        tail = ref[pl.ds(3 * B, TAIL), :].astype(f32)
        scale_ref[pl.ds(q * B, B), :] = column(tail[0:1, :] + tail[1:2, :])


def tile_product(kept_ref, group, slot, count, field):
    lhs = jnp.concatenate(
        [
            jnp.concatenate(
                [kept_ref[(group * GROUP + a) * SLOTS + slot + b] for b in range(GROUP * count)],
                axis=1,
            )
            for a in range(GROUP)
        ],
        axis=0,
    )
    return jnp.dot(lhs, field, preferred_element_type=f32)


def side_product(kept_ref, upper, m, field_ref):
    group = jnp.where(upper, m, TILE_ROWS - 1 - m)
    start = pl.multiple_of(jnp.where(upper, 0, TILE * (TILE_ROWS - 1 - m)), TILE)
    slot = jnp.where(upper, GROUP * (2 * TILE_ROWS - m), 0)
    field = field_ref[pl.ds(start, TILE * (m + 1)), :]
    return group, tile_product(kept_ref, group, slot, m + 1, field)


def near_products(kept_ref, own_ref, near_ref, first, second, ready=None):
    @pl.loop(0, TILE_ROWS)
    def _(group):
        if ready is not None:
            ready(group)
        part = tile_product(
            kept_ref, group, GROUP * (TILE_ROWS - group), TILE_ROWS, own_ref[pl.ds(0, FIELD), :]
        )
        first(pl.ds(pl.multiple_of(group * TILE, TILE), TILE), part)

    upper = core_of() == 0
    for m in range(TILE_ROWS):
        group, part = side_product(kept_ref, upper, m, near_ref)
        second(pl.ds(pl.multiple_of(group * TILE, TILE), TILE), part)


def far_products(kept_ref, far_ref, emit):
    upper = core_of() == 1
    for m in range(TILE_ROWS):
        group, part = side_product(kept_ref, upper, m, far_ref)
        emit(pl.ds(pl.multiple_of(group * TILE, TILE), TILE), part)


def sweep_near(kept_ref, own_ref, near_ref, x_ref, first_ref, ratio_ref, base_ref, ready=None):
    def first(rows, part):
        base_ref[rows, :] = (1.0 - RELAX) * x_ref[rows, :] + first_ref[rows, :] - ratio_ref[rows, :] * part

    def second(rows, part):
        base_ref[rows, :] -= ratio_ref[rows, :] * part

    near_products(kept_ref, own_ref, near_ref, first, second, ready)


def sweep_near_kernel(kept_ref, own_ref, near_ref, x_ref, first_ref, ratio_ref, base_ref):
    sweep_near(kept_ref, own_ref, near_ref, x_ref, first_ref, ratio_ref, base_ref)


def load_near_kernel(
    columns_ref, blocks_ref, own_ref, near_ref, x_ref, first_ref, ratio_ref, kept_ref, base_ref, sems
):
    first = lax.axis_index("rows") * ROWS - ROWS
    empty = jnp.zeros((B, B), bf16)

    @pl.loop(0, ROWS)
    def _(r):
        lead = lax.rem(r, GROUP)
        sem = sems.at[lax.div(r, GROUP)]
        base = r * SLOTS
        total = jnp.int32(0)
        for k in range(2 * ROWS):
            offset = jnp.bitwise_and(columns_ref[r, k] - first - r + 512, 511)
            offset = jnp.minimum(offset, 2 * ROWS)
            pltpu.make_async_copy(blocks_ref.at[r, k], kept_ref.at[base + lead + offset], sem).start()
            total = total + offset
        missing = jnp.clip(ROWS * (2 * ROWS + 1) - total, 0, 2 * ROWS)
        kept_ref[base + lead + missing] = empty
        for pad in range(GROUP - 1):
            place = jnp.where(pad < lead, pad, 2 * ROWS + 1 + pad)
            kept_ref[base + place] = empty

    def ready(group):
        for a in range(GROUP):
            r = group * GROUP + a
            pltpu.make_async_copy(
                blocks_ref.at[r], kept_ref.at[pl.ds(r * 2 * ROWS, 2 * ROWS)], sems.at[group]
            ).wait()

    sweep_near(kept_ref, own_ref, near_ref, x_ref, first_ref, ratio_ref, base_ref, ready)


def sweep_far_kernel(kept_ref, far_ref, base_ref, ratio_ref, x_ref, sent_ref):
    def emit(rows, part):
        value = base_ref[rows, :] - ratio_ref[rows, :] * part
        x_ref[rows, :] = value
        sent_ref[rows, :] = value.astype(bf16)

    far_products(kept_ref, far_ref, emit)


def last_far_kernel(kept_ref, far_ref, base_ref, ratio_ref, x_ref, x_s, sems):
    copies = []

    def emit(rows, part):
        x_s[rows, :] = base_ref[rows, :] - ratio_ref[rows, :] * part
        copy = pltpu.make_async_copy(x_s.at[rows, :], x_ref.at[rows, :], sems.at[len(copies)])
        copy.start()
        copies.append(copy)

    far_products(kept_ref, far_ref, emit)
    for copy in copies:
        copy.wait()


def residual_near_kernel(kept_ref, own_ref, near_ref, x_ref, right_ref, diag_ref, base_ref):
    def first(rows, part):
        base_ref[rows, :] = right_ref[rows, :] - diag_ref[rows, :] * x_ref[rows, :] - part

    def second(rows, part):
        base_ref[rows, :] -= part

    near_products(kept_ref, own_ref, near_ref, first, second)


def residual_far_kernel(kept_ref, group_ref, far_ref, base_ref, scale_ref, res_ref, side_ref, sent_ref):
    def emit(rows, part):
        res_ref[rows, :] = base_ref[rows, :] - part

    far_products(kept_ref, far_ref, emit)
    side_ref[...] = jnp.zeros((QROWS, B), f32)
    for r in range(ROWS):
        rows = pl.ds(pl.multiple_of(lax.div(group_ref[r], lax.axis_size("rows")) * B, B), B)
        side_ref[rows, :] += res_ref[pl.ds(r * B, B), :]
    value = scale_ref[...] * side_ref[...]
    side_ref[...] = value
    sent_ref[...] = value.astype(bf16)


def spread(coarse_ref, tail_ref, out_ref):
    tail = tail_ref[pl.ds(FIELD, TAIL), :].astype(f32)
    parts = [coarse_ref[pl.ds(q * B, B), :].astype(f32) for q in range(4)]
    for r in range(ROWS):
        group = tail[r : r + 1, :]
        value = jnp.where(group < 0.5, parts[0], parts[1])
        value = jnp.where(group < 1.5, value, parts[2])
        value = jnp.where(group < 2.5, value, parts[3])
        out_ref[pl.ds(r * B, B), :] = value.astype(bf16)


def lift_near_kernel(
    kept_ref, group_ref, coarse_ref, near_ref, near_tail_ref, x_ref, res_ref, ratio_ref, base_ref, own_s, near_s
):
    for r in range(ROWS):
        rows = pl.ds(pl.multiple_of(lax.div(group_ref[r], lax.axis_size("rows")) * B, B), B)
        own_s[pl.ds(r * B, B), :] = coarse_ref[rows, :]
    spread(near_ref, near_tail_ref, near_s)

    def first(rows, part):
        base_ref[rows, :] = (
            x_ref[rows, :]
            + (1.0 - RELAX) * own_s[rows, :].astype(f32)
            + ratio_ref[rows, :] * (res_ref[rows, :] - part)
        )

    def second(rows, part):
        base_ref[rows, :] -= ratio_ref[rows, :] * part

    near_products(kept_ref, own_s, near_s, first, second)


def lift_far_kernel(kept_ref, far_ref, far_tail_ref, base_ref, ratio_ref, x_ref, sent_ref, far_s):
    spread(far_ref, far_tail_ref, far_s)
    sweep_far_kernel(kept_ref, far_s, base_ref, ratio_ref, x_ref, sent_ref)


def coarse_terms(ops_ref, own_ref, near_ref, far_ref, emit):
    i = lax.axis_index("rows")
    last = lax.axis_size("rows") - 1
    near_is_upper = (core_of() == 0).astype(f32)
    step_up = (i == last).astype(jnp.int32)
    step_down = (i == 0).astype(jnp.int32)
    for q in range(4):
        at_up = pl.multiple_of(jnp.minimum(q + step_up, 3) * B, B)
        at_down = pl.multiple_of(jnp.maximum(q - step_down, 0) * B, B)
        keep_up = (q + step_up <= 3).astype(f32)
        keep_down = (q - step_down >= 0).astype(f32)
        upper = near_is_upper * near_ref[pl.ds(at_up, B), :].astype(f32) + (
            1.0 - near_is_upper
        ) * far_ref[pl.ds(at_up, B), :].astype(f32)
        lower = near_is_upper * far_ref[pl.ds(at_down, B), :].astype(f32) + (
            1.0 - near_is_upper
        ) * near_ref[pl.ds(at_down, B), :].astype(f32)
        field = jnp.concatenate(
            [
                (keep_down * lower).astype(bf16),
                own_ref[pl.ds(q * B, B), :],
                (keep_up * upper).astype(bf16),
            ],
            axis=0,
        )
        ops = jnp.concatenate([ops_ref[q * 3 + d] for d in range(3)], axis=1)
        emit(pl.ds(q * B, B), jnp.dot(ops, field, preferred_element_type=f32))


def ratios():
    sigma = THETA / DELTA
    old = 1.0 / sigma
    out = []
    for _ in range(CHEB - 1):
        new = 1.0 / (2.0 * sigma - old)
        out.append((new * old, 2.0 * new / DELTA))
        old = new
    return out


def coarse_first_kernel(ops_ref, side_ref, own_ref, near_ref, far_ref, fix_ref, sent_ref):
    keep, gain = ratios()[0]

    def emit(rows, part):
        side = side_ref[rows, :] / THETA
        fix = side + keep * side + gain * (side_ref[rows, :] - side - part)
        fix_ref[rows, :] = fix
        sent_ref[rows, :] = fix.astype(bf16)

    coarse_terms(ops_ref, own_ref, near_ref, far_ref, emit)


def coarse_second_kernel(ops_ref, side_ref, fix_ref, own_ref, near_ref, far_ref, sent_ref):
    keep, gain = ratios()[1]

    def emit(rows, part):
        fix = fix_ref[rows, :]
        update = fix - side_ref[rows, :] / THETA
        fix = fix + keep * update + gain * (side_ref[rows, :] - fix - part)
        sent_ref[rows, :] = fix.astype(bf16)

    coarse_terms(ops_ref, own_ref, near_ref, far_ref, emit)


def run(kernel, outs, args, scratch=(), cost=(0, 0), to_hbm=False):
    specs, values = [], []
    for value, space in args:
        if space == "v":
            specs.append(VMEM_SPEC)
            values.append(resident(value))
        elif space == "b":
            specs.append(VMEM_SPEC)
            values.append(value)
        elif space == "s":
            specs.append(SMEM_SPEC)
            values.append(value)
        else:
            specs.append(ANY_SPEC)
            values.append(pltpu.with_memory_space_constraint(value, pltpu.HBM))
    return pl.pallas_call(
        kernel,
        out_shape=[
            jax.ShapeDtypeStruct(shape, dtype) if to_hbm else pltpu.VMEM(shape, dtype)
            for shape, dtype in outs
        ],
        in_specs=specs,
        out_specs=[ANY_SPEC if to_hbm else VMEM_SPEC] * len(outs),
        scratch_shapes=list(scratch),
        cost_estimate=pl.CostEstimate(flops=cost[0], bytes_accessed=cost[1], transcendentals=0),
        compiler_params=pltpu.CompilerParams(vmem_limit_bytes=LIMIT),
    )(*values)


def swap(x, size):
    far = lax.ppermute(
        x, "rows", [(i, (i - 1) % size if i % 2 == 0 else (i + 1) % size) for i in range(size)]
    )
    near = lax.ppermute(x, "rows", [(i, i ^ 1) for i in range(size)])
    return near, far


FULL = (FIELD, B)
SIDE = (QROWS, B)
NEAR_COST = (2 * 26 * TILE * TILE * B, 8_000_000)
FAR_COST = (2 * 10 * TILE * TILE * B, 3_000_000)


def shards(right_side, fine_blocks, fine_columns, fine_diag, aggregate, coarse_blocks, coarse_diag):
    size = lax.axis_size("rows")
    group = aggregate

    first, sent, ratio, diag = run(
        start_kernel,
        [(FULL, f32), ((FIELD + TAIL, B), bf16), (FULL, f32), (FULL, f32)],
        [(right_side, "h"), (fine_diag.reshape(ROWS, B), "h"), (group, "h")],
        [
            pltpu.VMEM(FULL, f32),
            pltpu.VMEM((ROWS, B), f32),
            pltpu.SMEM((ROWS,), jnp.int32),
            pltpu.SemaphoreType.DMA((TILE_ROWS + 2,)),
        ],
    )
    near, far = swap(sent, size)
    near_tail, far_tail = near, far
    kept, base = run(
        load_near_kernel,
        [((ROWS * SLOTS, B, B), bf16), (FULL, f32)],
        [
            (fine_columns, "s"), (fine_blocks, "h"), (sent, "v"), (near, "v"), (first, "v"),
            (first, "v"), (ratio, "v"),
        ],
        [pltpu.SemaphoreType.DMA((TILE_ROWS,))],
        (NEAR_COST[0], 28_000_000),
    )
    (packed,) = run(
        pack_kernel,
        [((3 * B + TAIL, B), bf16)],
        [(coarse_blocks, "b"), (coarse_diag.reshape(1, B), "b")],
    )
    pieces = [packed] + [
        lax.ppermute(packed, "rhs", [(i, (i + k) % 4) for i in range(4)]) for k in range(1, 4)
    ]
    def sweep_start(x, sent, near):
        return run(
            sweep_near_kernel,
            [(FULL, f32)],
            [(kept, "v"), (sent, "v"), (near, "v"), (x, "v"), (first, "v"), (ratio, "v")],
            cost=NEAR_COST,
        )[0]

    def sweep_end(far, base):
        return run(
            sweep_far_kernel,
            [(FULL, f32), (FULL, bf16)],
            [(kept, "v"), (far, "v"), (base, "v"), (ratio, "v")],
            cost=FAR_COST,
        )

    x = first
    for turn in range(CYCLES):
        for _ in range(2 * (turn > 0)):
            near, far = swap(sent, size)
            base = sweep_start(x, sent, near)
            x, sent = sweep_end(far, base)
        if turn == 0:
            x, sent = sweep_end(far, base)
        near, far = swap(sent, size)
        (base,) = run(
            residual_near_kernel,
            [(FULL, f32)],
            [(kept, "v"), (sent, "v"), (near, "v"), (x, "v"), (right_side, "b"), (diag, "v")],
            cost=NEAR_COST,
        )
        if turn == 0:
            ops, scale = run(
                sort_kernel,
                [((12, B, B), bf16), (SIDE, f32)],
                [(p, "v") for p in pieces] + [(base, "v")],
            )
        res, side, sent = run(
            residual_far_kernel,
            [(FULL, f32), (SIDE, f32), (SIDE, bf16)],
            [(kept, "v"), (group, "s"), (far, "v"), (base, "v"), (scale, "v")],
            cost=FAR_COST,
        )
        near, far = swap(sent, size)
        fix, sent = run(
            coarse_first_kernel,
            [(SIDE, f32), (SIDE, bf16)],
            [(ops, "v"), (side, "v"), (sent, "v"), (near, "v"), (far, "v")],
        )
        near, far = swap(sent, size)
        (sent,) = run(
            coarse_second_kernel,
            [(SIDE, bf16)],
            [(ops, "v"), (side, "v"), (fix, "v"), (sent, "v"), (near, "v"), (far, "v")],
        )
        near, far = swap(sent, size)
        (base,) = run(
            lift_near_kernel,
            [(FULL, f32)],
            [
                (kept, "v"), (group, "s"), (sent, "v"), (near, "v"), (near_tail, "v"),
                (x, "v"), (res, "v"), (ratio, "v"),
            ],
            [pltpu.VMEM(FULL, bf16), pltpu.VMEM(FULL, bf16)],
            NEAR_COST,
        )
        x, sent = run(
            lift_far_kernel,
            [(FULL, f32), (FULL, bf16)],
            [(kept, "v"), (far, "v"), (far_tail, "v"), (base, "v"), (ratio, "v")],
            [pltpu.VMEM(FULL, bf16)],
            FAR_COST,
        )
        near, far = swap(sent, size)
        base = sweep_start(x, sent, near)
        if turn < CYCLES - 1:
            x, sent = sweep_end(far, base)
    (x,) = run(
        last_far_kernel,
        [(FULL, f32)],
        [(kept, "v"), (far, "v"), (base, "v"), (ratio, "v")],
        [pltpu.VMEM(FULL, f32), pltpu.SemaphoreType.DMA((TILE_ROWS,))],
        FAR_COST,
        to_hbm=True,
    )
    return x


def solution(mesh):
    in_specs = (
        P("rows", "rhs"),
        P("rows", None, None, None),
        P("rows", None),
        P("rows"),
        P("rows"),
        P(("rhs", "rows"), None, None, None),
        P(("rhs", "rows")),
    )
    return jax.shard_map(
        shards, mesh=mesh, in_specs=in_specs, out_specs=P("rows", "rhs"), check_vma=False
    )
```

```python
import functools

import jax
import jax.numpy as jnp
from jax import lax
from jax.experimental import pallas as pl
from jax.experimental.pallas import tpu as pltpu
from jax.sharding import PartitionSpec as P

CYCLES = 2
CHEB = 3
RELAX = 0.7
THETA = 1.0
DELTA = 0.6

B = 128
ROWS = 16
GROUP = 4
TILE = GROUP * B
TILE_ROWS = ROWS // GROUP
SLOTS = 36
FIELD = ROWS * B
TAIL = 16
QROWS = 4 * B
PIECE = 3 * TILE

f32 = jnp.float32
bf16 = jnp.bfloat16
VMEM_SPEC = pl.BlockSpec(memory_space=pltpu.VMEM)
SMEM_SPEC = pl.BlockSpec(memory_space=pltpu.SMEM)
ANY_SPEC = pl.BlockSpec(memory_space=pl.ANY)
LIMIT = 12 * 1024 * 1024


def resident(x):
    return pltpu.with_memory_space_constraint(x, pltpu.VMEM)


def core_of():
    return lax.rem(lax.axis_index("rows"), 2)


def column(row):
    return jnp.transpose(jnp.broadcast_to(row, (B, B)))


def places(columns_ref, out_ref):
    row = lax.broadcasted_iota(jnp.int32, (ROWS, 2 * ROWS), 0)
    first = lax.axis_index("rows") * ROWS - ROWS
    offset = jnp.bitwise_and(columns_ref[...] - first - row + 512, 511)
    offset = jnp.minimum(offset, 2 * ROWS)
    start = row * SLOTS + jnp.bitwise_and(row, GROUP - 1)
    missing = ROWS * (2 * ROWS + 1) - jnp.sum(offset, axis=1, keepdims=True)
    missing = jnp.clip(missing, 0, 2 * ROWS) + start[:, 0:1]
    out_ref[:, 0 : 2 * ROWS] = start + offset
    out_ref[:, 2 * ROWS : B] = jnp.broadcast_to(missing, (ROWS, B - 2 * ROWS))


def start_kernel(
    right_ref, diag_ref, group_ref, coarse_ref, coarse_diag_ref, columns_ref,
    first_ref, sent_ref, head_ref, rest_ref, ratio_ref, diag_out_ref, packed_ref, places_ref,
    right_s, diag_s, group_s, coarse_s, coarse_diag_s, columns_s, sems,
):
    chunks = [
        pltpu.make_async_copy(
            right_ref.at[pl.ds(g * TILE, TILE), :], right_s.at[pl.ds(g * TILE, TILE), :], sems.at[g]
        )
        for g in range(TILE_ROWS)
    ]
    diag_copy = pltpu.make_async_copy(diag_ref, diag_s, sems.at[TILE_ROWS])
    group_copy = pltpu.make_async_copy(group_ref, group_s, sems.at[TILE_ROWS + 1])
    coarse_copy = pltpu.make_async_copy(coarse_ref, coarse_s, sems.at[TILE_ROWS + 2])
    coarse_diag_copy = pltpu.make_async_copy(coarse_diag_ref, coarse_diag_s, sems.at[TILE_ROWS + 3])
    columns_copy = pltpu.make_async_copy(columns_ref, columns_s, sems.at[TILE_ROWS + 4])
    columns_copy.start()
    coarse_diag_copy.start()
    coarse_copy.start()
    diag_copy.start()
    for chunk in chunks:
        chunk.start()
    group_copy.start()
    columns_copy.wait()
    places(columns_s, places_ref)
    coarse_diag_copy.wait()
    coarse_copy.wait()
    pack(coarse_s, coarse_diag_s, packed_ref)
    diag_copy.wait()
    for g in range(TILE_ROWS):
        chunks[g].wait()
        for r in range(g * GROUP, (g + 1) * GROUP):
            rows = pl.ds(r * B, B)
            diag = column(diag_s[r : r + 1, :])
            ratio = RELAX / diag
            value = ratio * right_s[rows, :]
            diag_out_ref[rows, :] = diag
            ratio_ref[rows, :] = ratio
            first_ref[rows, :] = value
            sent_ref[rows, :] = value.astype(bf16)
    even = core_of() == 0
    head = pl.multiple_of(jnp.where(even, 0, TILE), TILE)
    rest = pl.multiple_of(jnp.where(even, PIECE, 0), TILE)
    head_ref[pl.ds(0, PIECE), :] = sent_ref[pl.ds(head, PIECE), :]
    rest_ref[...] = sent_ref[pl.ds(rest, TILE), :]
    group_copy.wait()
    size = lax.axis_size("rows")
    index = lax.broadcasted_iota(jnp.int32, (TAIL, B), 0)
    tail = jnp.zeros((TAIL, B), f32)
    for r in range(ROWS):
        tail = jnp.where(index == r, lax.div(group_s[r], size).astype(f32), tail)
    sent_ref[pl.ds(FIELD, TAIL), :] = tail.astype(bf16)
    head_ref[pl.ds(PIECE, TAIL), :] = tail.astype(bf16)


def pack(blocks_ref, diag_ref, out_ref):
    inverse = 1.0 / diag_ref[...]
    scale = column(inverse)
    for d in range(3):
        out_ref[pl.ds(d * B, B), :] = (scale * blocks_ref[0, d]).astype(bf16)
    high = inverse.astype(bf16).astype(f32)
    low = inverse - high
    index = lax.broadcasted_iota(jnp.int32, (TAIL, B), 0)
    out_ref[pl.ds(3 * B, TAIL), :] = jnp.where(index == 0, high, low).astype(bf16)


def sort_kernel(p0_ref, p1_ref, p2_ref, p3_ref, after_ref, ops_ref, scale_ref):
    me = lax.axis_index("rhs")
    for k, ref in enumerate((p0_ref, p1_ref, p2_ref, p3_ref)):
        q = jnp.bitwise_and(me - k + 4, 3)
        for d in range(3):
            ops_ref[q * 3 + d] = ref[pl.ds(d * B, B), :]
        tail = ref[pl.ds(3 * B, TAIL), :].astype(f32)
        scale_ref[pl.ds(q * B, B), :] = column(tail[0:1, :] + tail[1:2, :])


def tile_product(kept_ref, group, slot, count, field):
    lhs = jnp.concatenate(
        [
            jnp.concatenate(
                [kept_ref[(group * GROUP + a) * SLOTS + slot + b] for b in range(GROUP * count)],
                axis=1,
            )
            for a in range(GROUP)
        ],
        axis=0,
    )
    return jnp.dot(lhs, field, preferred_element_type=f32)


def rows_of(group):
    return pl.ds(pl.multiple_of(group * TILE, TILE), TILE)


def field_at(ref, tile, count):
    return ref[pl.ds(pl.multiple_of(tile * TILE, TILE), count * TILE), :]


def group_of(upper, m):
    return jnp.where(upper, m, TILE_ROWS - 1 - m)


def side_slot(upper, m, j):
    return jnp.where(upper, GROUP * (2 * TILE_ROWS - m + j), GROUP * j)


def near_products(kept_ref, own_ref, near_ref, first, second, straight=False, ready=None):
    @pl.loop(0, TILE_ROWS)
    def _(group):
        if ready is not None:
            ready(group)
        part = tile_product(
            kept_ref, group, GROUP * (TILE_ROWS - group), TILE_ROWS, own_ref[pl.ds(0, FIELD), :]
        )
        first(rows_of(group), part)

    upper = core_of() == 0

    def side(m, j, count):
        group = group_of(upper, m)
        field = field_at(near_ref, jnp.where(upper, j, TILE_ROWS - 1 - m + j), count)
        second(rows_of(group), tile_product(kept_ref, group, side_slot(upper, m, j), count, field))

    if straight:
        for m in range(TILE_ROWS):
            side(m, 0, m + 1)
        return

    @pl.loop(0, 4)
    def _(p):
        side(jnp.minimum(p + 1, 3), jnp.where(p == 3, 2, 0), 2)

    @pl.loop(0, 2)
    def _(p):
        side(2 * p, 2 * p, 1)


def far_products(kept_ref, far_ref, emit):
    upper = core_of() == 1
    for m in range(TILE_ROWS):
        group = group_of(upper, m)
        field = field_at(far_ref, jnp.where(upper, 0, TILE_ROWS - 1 - m), m + 1)
        emit(m, rows_of(group), tile_product(kept_ref, group, side_slot(upper, m, 0), m + 1, field))


def head_products(kept_ref, head_ref, emit):
    upper = core_of() == 1
    for m in range(TILE_ROWS - 1):
        group = group_of(upper, m)
        field = field_at(head_ref, jnp.where(upper, 0, TILE_ROWS - 2 - m), m + 1)
        emit(m, rows_of(group), tile_product(kept_ref, group, side_slot(upper, m, 0), m + 1, field))
    m = TILE_ROWS - 1
    group = group_of(upper, m)
    slot = jnp.where(upper, side_slot(True, m, 0), side_slot(False, m, 1))
    emit(m, rows_of(group), tile_product(kept_ref, group, slot, m, field_at(head_ref, 0, m)))


def rest_product(kept_ref, rest_ref):
    upper = core_of() == 1
    m = TILE_ROWS - 1
    group = group_of(upper, m)
    slot = jnp.where(upper, side_slot(True, m, m), side_slot(False, m, 0))
    return rows_of(group), tile_product(kept_ref, group, slot, 1, rest_ref[...])


def send(m, rows, value, sent_ref, head_ref, rest_ref):
    value = value.astype(bf16)
    sent_ref[rows, :] = value
    if m == 0:
        rest_ref[...] = value
    else:
        at = jnp.where(core_of() == 1, m - 1, TILE_ROWS - 1 - m)
        head_ref[rows_of(at), :] = value


def sweep_near(
    kept_ref, own_ref, near_ref, x_ref, first_ref, ratio_ref, base_ref, straight=False, ready=None
):
    def first(rows, part):
        base_ref[rows, :] = (1.0 - RELAX) * x_ref[rows, :] + first_ref[rows, :] - ratio_ref[rows, :] * part

    def second(rows, part):
        base_ref[rows, :] -= ratio_ref[rows, :] * part

    near_products(kept_ref, own_ref, near_ref, first, second, straight, ready)


def sweep_near_kernel(kept_ref, own_ref, near_ref, x_ref, first_ref, ratio_ref, base_ref):
    sweep_near(kept_ref, own_ref, near_ref, x_ref, first_ref, ratio_ref, base_ref)


def load_near_kernel(
    places_ref, blocks_ref, own_ref, near_ref, first_ref, ratio_ref, kept_ref, base_ref, sems
):
    empty = jnp.zeros((B, B), bf16)

    @pl.loop(0, ROWS)
    def _(r):
        sem = sems.at[lax.div(r, GROUP)]
        for k in range(2 * ROWS):
            pltpu.make_async_copy(blocks_ref.at[r, k], kept_ref.at[places_ref[r, k]], sem).start()

    for r in range(ROWS):
        lead = r % GROUP
        kept_ref[places_ref[r, 2 * ROWS]] = empty
        for pad in range(GROUP - 1):
            kept_ref[r * SLOTS + (pad if pad < lead else 2 * ROWS + 1 + pad)] = empty

    def ready(group):
        for a in range(GROUP):
            r = group * GROUP + a
            pltpu.make_async_copy(
                blocks_ref.at[r], kept_ref.at[pl.ds(r * 2 * ROWS, 2 * ROWS)], sems.at[group]
            ).wait()

    sweep_near(
        kept_ref, own_ref, near_ref, first_ref, first_ref, ratio_ref, base_ref, True, ready
    )


def sweep_head_kernel(kept_ref, far_ref, base_ref, ratio_ref, x_ref, sent_ref, head_ref, rest_ref):
    def emit(m, rows, part):
        value = base_ref[rows, :] - ratio_ref[rows, :] * part
        x_ref[rows, :] = value
        if m < TILE_ROWS - 1:
            send(m, rows, value, sent_ref, head_ref, rest_ref)

    head_products(kept_ref, far_ref, emit)


def sweep_rest_kernel(
    kept_ref, far_ref, ratio_ref, x_in, sent_in, head_in, x_ref, sent_ref, head_ref
):
    rows, part = rest_product(kept_ref, far_ref)
    value = x_in[rows, :] - ratio_ref[rows, :] * part
    x_ref[rows, :] = value
    send(TILE_ROWS - 1, rows, value, sent_ref, head_ref, None)


def last_head_kernel(kept_ref, far_ref, base_ref, ratio_ref, x_ref):
    def emit(m, rows, part):
        x_ref[rows, :] = base_ref[rows, :] - ratio_ref[rows, :] * part

    head_products(kept_ref, far_ref, emit)


def last_rest_kernel(kept_ref, far_ref, ratio_ref, x_in, x_ref, x_s, sems):
    upper = core_of() == 1
    copies = []
    for m in range(TILE_ROWS - 1):
        done = rows_of(group_of(upper, m))
        copies.append(pltpu.make_async_copy(x_in.at[done, :], x_ref.at[done, :], sems.at[m]))
        copies[m].start()
    rows, part = rest_product(kept_ref, far_ref)
    x_s[...] = x_in[rows, :] - ratio_ref[rows, :] * part
    copies.append(pltpu.make_async_copy(x_s, x_ref.at[rows, :], sems.at[TILE_ROWS - 1]))
    copies[-1].start()
    for copy in copies:
        copy.wait()


def residual_near_kernel(
    straight, kept_ref, own_ref, near_ref, x_ref, right_ref, diag_ref, base_ref
):
    def first(rows, part):
        base_ref[rows, :] = right_ref[rows, :] - diag_ref[rows, :] * x_ref[rows, :] - part

    def second(rows, part):
        base_ref[rows, :] -= part

    near_products(kept_ref, own_ref, near_ref, first, second, straight)


def residual_head_kernel(kept_ref, group_ref, far_ref, base_ref, res_ref, side_ref):
    side_ref[...] = jnp.zeros((QROWS, B), f32)
    upper = core_of() == 1

    def emit(m, rows, part):
        value = base_ref[rows, :] - part
        res_ref[rows, :] = value
        if m < TILE_ROWS - 1:
            for a in range(GROUP):
                group = lax.div(group_ref[group_of(upper, m) * GROUP + a], lax.axis_size("rows"))
                side_ref[pl.ds(pl.multiple_of(group * B, B), B), :] += value[a * B : (a + 1) * B, :]

    head_products(kept_ref, far_ref, emit)


def residual_far_kernel(
    kept_ref, group_ref, far_ref, base_ref, scale_ref, res_ref, side_ref, sent_ref
):
    upper = core_of() == 1
    side_ref[...] = jnp.zeros((QROWS, B), f32)

    def emit(m, rows, part):
        value = base_ref[rows, :] - part
        res_ref[rows, :] = value
        for a in range(GROUP):
            group = lax.div(group_ref[group_of(upper, m) * GROUP + a], lax.axis_size("rows"))
            side_ref[pl.ds(pl.multiple_of(group * B, B), B), :] += value[a * B : (a + 1) * B, :]

    far_products(kept_ref, far_ref, emit)
    value = scale_ref[...] * side_ref[...]
    side_ref[...] = value
    sent_ref[...] = value.astype(bf16)


def residual_rest_kernel(
    kept_ref, tail_ref, far_ref, scale_ref, res_in, side_in, res_ref, side_ref, sent_ref
):
    upper = (core_of() == 1).astype(f32)
    tail = tail_ref[pl.ds(FIELD, TAIL), :].astype(f32)
    rows, part = rest_product(kept_ref, far_ref)
    value = res_in[rows, :] - part
    res_ref[rows, :] = value
    for q in range(4):
        place = pl.ds(q * B, B)
        total = side_in[place, :]
        for a in range(GROUP):
            at = TAIL - GROUP + a
            group = upper * tail[at : at + 1, :] + (1.0 - upper) * tail[a : a + 1, :]
            total = total + jnp.where(group == q, 1.0, 0.0) * value[a * B : (a + 1) * B, :]
        total = scale_ref[place, :] * total
        side_ref[place, :] = total
        sent_ref[place, :] = total.astype(bf16)


def spread(coarse_ref, tail_ref, start, out_ref):
    tail = tail_ref[pl.ds(start, TAIL), :].astype(f32)
    parts = [coarse_ref[pl.ds(q * B, B), :].astype(f32) for q in range(4)]
    for r in range(ROWS):
        group = tail[r : r + 1, :]
        value = jnp.where(group < 0.5, parts[0], parts[1])
        value = jnp.where(group < 1.5, value, parts[2])
        value = jnp.where(group < 2.5, value, parts[3])
        out_ref[pl.ds(r * B, B), :] = value.astype(bf16)


def lift_near_kernel(
    kept_ref, group_ref, coarse_ref, near_ref, near_tail_ref, x_ref, res_ref, ratio_ref, base_ref, own_s, near_s
):
    for r in range(ROWS):
        rows = pl.ds(pl.multiple_of(lax.div(group_ref[r], lax.axis_size("rows")) * B, B), B)
        own_s[pl.ds(r * B, B), :] = coarse_ref[rows, :]
    spread(near_ref, near_tail_ref, FIELD, near_s)

    def first(rows, part):
        base_ref[rows, :] = (
            x_ref[rows, :]
            + (1.0 - RELAX) * own_s[rows, :].astype(f32)
            + ratio_ref[rows, :] * (res_ref[rows, :] - part)
        )

    def second(rows, part):
        base_ref[rows, :] -= ratio_ref[rows, :] * part

    near_products(kept_ref, own_s, near_s, first, second)


def lift_far_kernel(
    kept_ref, far_ref, far_tail_ref, base_ref, ratio_ref, x_ref, sent_ref, head_ref, rest_ref, far_s
):
    spread(far_ref, far_tail_ref, PIECE, far_s)

    def emit(m, rows, part):
        value = base_ref[rows, :] - ratio_ref[rows, :] * part
        x_ref[rows, :] = value
        send(m, rows, value, sent_ref, head_ref, rest_ref)

    far_products(kept_ref, far_s, emit)


def coarse_terms(ops_ref, own_ref, near_ref, far_ref, emit):
    i = lax.axis_index("rows")
    last = lax.axis_size("rows") - 1
    near_is_upper = (core_of() == 0).astype(f32)
    step_up = (i == last).astype(jnp.int32)
    step_down = (i == 0).astype(jnp.int32)
    for q in range(4):
        at_up = pl.multiple_of(jnp.minimum(q + step_up, 3) * B, B)
        at_down = pl.multiple_of(jnp.maximum(q - step_down, 0) * B, B)
        keep_up = (q + step_up <= 3).astype(f32)
        keep_down = (q - step_down >= 0).astype(f32)
        upper = near_is_upper * near_ref[pl.ds(at_up, B), :].astype(f32) + (
            1.0 - near_is_upper
        ) * far_ref[pl.ds(at_up, B), :].astype(f32)
        lower = near_is_upper * far_ref[pl.ds(at_down, B), :].astype(f32) + (
            1.0 - near_is_upper
        ) * near_ref[pl.ds(at_down, B), :].astype(f32)
        field = jnp.concatenate(
            [
                (keep_down * lower).astype(bf16),
                own_ref[pl.ds(q * B, B), :],
                (keep_up * upper).astype(bf16),
            ],
            axis=0,
        )
        ops = jnp.concatenate([ops_ref[q * 3 + d] for d in range(3)], axis=1)
        emit(pl.ds(q * B, B), jnp.dot(ops, field, preferred_element_type=f32))


def ratios():
    sigma = THETA / DELTA
    old = 1.0 / sigma
    out = []
    for _ in range(CHEB - 1):
        new = 1.0 / (2.0 * sigma - old)
        out.append((new * old, 2.0 * new / DELTA))
        old = new
    return out


def coarse_first_kernel(ops_ref, side_ref, own_ref, near_ref, far_ref, fix_ref, sent_ref):
    keep, gain = ratios()[0]

    def emit(rows, part):
        side = side_ref[rows, :] / THETA
        fix = side + keep * side + gain * (side_ref[rows, :] - side - part)
        fix_ref[rows, :] = fix
        sent_ref[rows, :] = fix.astype(bf16)

    coarse_terms(ops_ref, own_ref, near_ref, far_ref, emit)


def coarse_second_kernel(ops_ref, side_ref, fix_ref, own_ref, near_ref, far_ref, sent_ref):
    keep, gain = ratios()[1]

    def emit(rows, part):
        fix = fix_ref[rows, :]
        update = fix - side_ref[rows, :] / THETA
        fix = fix + keep * update + gain * (side_ref[rows, :] - fix - part)
        sent_ref[rows, :] = fix.astype(bf16)

    coarse_terms(ops_ref, own_ref, near_ref, far_ref, emit)


def run(kernel, outs, args, scratch=(), cost=(0, 0), hbm_outs=(), alias={}):
    specs, values = [], []
    for value, space in args:
        if space == "v":
            specs.append(VMEM_SPEC)
            values.append(resident(value))
        elif space == "b":
            specs.append(VMEM_SPEC)
            values.append(value)
        elif space == "s":
            specs.append(SMEM_SPEC)
            values.append(value)
        elif space == "a":
            specs.append(ANY_SPEC)
            values.append(value)
        else:
            specs.append(ANY_SPEC)
            values.append(pltpu.with_memory_space_constraint(value, pltpu.HBM))
    return pl.pallas_call(
        kernel,
        out_shape=[
            jax.ShapeDtypeStruct(shape, dtype) if n in hbm_outs else pltpu.VMEM(shape, dtype)
            for n, (shape, dtype) in enumerate(outs)
        ],
        in_specs=specs,
        out_specs=[ANY_SPEC if n in hbm_outs else VMEM_SPEC for n in range(len(outs))],
        input_output_aliases=alias,
        scratch_shapes=list(scratch),
        cost_estimate=pl.CostEstimate(flops=cost[0], bytes_accessed=cost[1], transcendentals=0),
        compiler_params=pltpu.CompilerParams(vmem_limit_bytes=LIMIT),
    )(*values)


def swap_near(x, size):
    return lax.ppermute(x, "rows", [(i, i ^ 1) for i in range(size)])


def swap_far(x, size):
    pairs = [(i, (i - 1) % size if i % 2 == 0 else (i + 1) % size) for i in range(size)]
    return lax.ppermute(x, "rows", pairs)


FULL = (FIELD, B)
HEAD = (PIECE, B)
REST = (TILE, B)
SIDE = (QROWS, B)
TILE_FLOPS = 2 * TILE * TILE * B
NEAR_COST = (26 * TILE_FLOPS, 8_000_000)
HEAD_COST = (9 * TILE_FLOPS, 3_000_000)
REST_COST = (TILE_FLOPS, 1_000_000)
FIELDS = [(FULL, f32), (FULL, bf16), (HEAD, bf16), (REST, bf16)]


def shards(right_side, fine_blocks, fine_columns, fine_diag, aggregate, coarse_blocks, coarse_diag):
    size = lax.axis_size("rows")

    first, sent, head, rest, ratio, diag, packed, places_of = run(
        start_kernel,
        [
            (FULL, f32), ((FIELD + TAIL, B), bf16), ((PIECE + TAIL, B), bf16), (REST, bf16),
            (FULL, f32), (FULL, f32), ((3 * B + TAIL, B), bf16),
            ((ROWS, B), jnp.int32),
        ],
        [
            (right_side, "h"), (fine_diag.reshape(ROWS, B), "h"), (aggregate, "h"),
            (coarse_blocks, "h"), (coarse_diag.reshape(1, B), "h"),
            (fine_columns, "h"),
        ],
        [
            pltpu.VMEM(FULL, f32),
            pltpu.VMEM((ROWS, B), f32),
            pltpu.SMEM((ROWS,), jnp.int32),
            pltpu.VMEM((1, 3, B, B), f32),
            pltpu.VMEM((1, B), f32),
            pltpu.VMEM((ROWS, 2 * ROWS), jnp.int32),
            pltpu.SemaphoreType.DMA((TILE_ROWS + 5,)),
        ],
    )

    def swap_fields(sent, head, rest):
        return swap_far(head, size), swap_far(rest, size), swap_near(sent, size)

    def swap_sides(sent):
        return swap_far(sent, size), swap_near(sent, size)

    pieces = [packed] + [
        lax.ppermute(packed, "rhs", [(i, (i + k) % 4) for i in range(4)]) for k in range(1, 4)
    ]
    far, far_rest, near = swap_fields(sent, head, rest)
    own_tail, near_tail, far_tail = sent, near, far
    kept, base = run(
        load_near_kernel,
        [((ROWS * SLOTS, B, B), bf16), (FULL, f32)],
        [
            (places_of, "s"), (fine_blocks, "h"), (sent, "v"), (near, "v"), (first, "v"),
            (ratio, "v"),
        ],
        [pltpu.SemaphoreType.DMA((TILE_ROWS,))],
        (NEAR_COST[0], 28_000_000),
    )

    def sweep_start(x, sent, near):
        return run(
            sweep_near_kernel,
            [(FULL, f32)],
            [(kept, "v"), (sent, "v"), (near, "v"), (x, "v"), (first, "v"), (ratio, "v")],
            cost=NEAR_COST,
        )[0]

    def sweep_end(far, far_rest, base):
        x, sent, head, rest = run(
            sweep_head_kernel,
            FIELDS,
            [(kept, "v"), (far, "v"), (base, "v"), (ratio, "v")],
            cost=HEAD_COST,
        )
        x, sent, head = run(
            sweep_rest_kernel,
            FIELDS[:3],
            [(kept, "v"), (far_rest, "v"), (ratio, "v"), (x, "v"), (sent, "v"), (head, "v")],
            cost=REST_COST,
            alias={3: 0, 4: 1, 5: 2},
        )
        return x, sent, head, rest

    x = first
    for turn in range(CYCLES):
        for _ in range(2 * (turn > 0)):
            far, far_rest, near = swap_fields(sent, head, rest)
            base = sweep_start(x, sent, near)
            x, sent, head, rest = sweep_end(far, far_rest, base)
        if turn == 0:
            x, sent, head, rest = sweep_end(far, far_rest, base)
        if turn == 0:
            far, near = swap_sides(sent)
        else:
            far, far_rest, near = swap_fields(sent, head, rest)
        (base,) = run(
            functools.partial(residual_near_kernel, turn == 0),
            [(FULL, f32)],
            [(kept, "v"), (sent, "v"), (near, "v"), (x, "v"), (right_side, "b"), (diag, "v")],
            cost=NEAR_COST,
        )
        if turn == 0:
            ops, scale = run(
                sort_kernel,
                [((12, B, B), bf16), (SIDE, f32)],
                [(p, "v") for p in pieces] + [(base, "v")],
            )
            res, side, sent = run(
                residual_far_kernel,
                [(FULL, f32), (SIDE, f32), (SIDE, bf16)],
                [(kept, "v"), (aggregate, "s"), (far, "v"), (base, "v"), (scale, "v")],
                cost=HEAD_COST,
            )
        else:
            res, side = run(
                residual_head_kernel,
                [(FULL, f32), (SIDE, f32)],
                [(kept, "v"), (aggregate, "s"), (far, "v"), (base, "v")],
                cost=HEAD_COST,
            )
            res, side, sent = run(
                residual_rest_kernel,
                [(FULL, f32), (SIDE, f32), (SIDE, bf16)],
                [
                    (kept, "v"), (own_tail, "v"), (far_rest, "v"), (scale, "v"), (res, "v"),
                    (side, "v"),
                ],
                cost=REST_COST,
                alias={4: 0, 5: 1},
            )
        far, near = swap_sides(sent)
        fix, sent = run(
            coarse_first_kernel,
            [(SIDE, f32), (SIDE, bf16)],
            [(ops, "v"), (side, "v"), (sent, "v"), (near, "v"), (far, "v")],
        )
        far, near = swap_sides(sent)
        (sent,) = run(
            coarse_second_kernel,
            [(SIDE, bf16)],
            [(ops, "v"), (side, "v"), (fix, "v"), (sent, "v"), (near, "v"), (far, "v")],
        )
        far, near = swap_sides(sent)
        (base,) = run(
            lift_near_kernel,
            [(FULL, f32)],
            [
                (kept, "v"), (aggregate, "s"), (sent, "v"), (near, "v"), (near_tail, "v"),
                (x, "v"), (res, "v"), (ratio, "v"),
            ],
            [pltpu.VMEM(FULL, bf16), pltpu.VMEM(FULL, bf16)],
            NEAR_COST,
        )
        x, sent, head, rest = run(
            lift_far_kernel,
            FIELDS,
            [(kept, "v"), (far, "v"), (far_tail, "v"), (base, "v"), (ratio, "v")],
            [pltpu.VMEM(FULL, bf16)],
            (10 * TILE_FLOPS, 3_000_000),
        )
        far, far_rest, near = swap_fields(sent, head, rest)
        base = sweep_start(x, sent, near)
        if turn < CYCLES - 1:
            x, sent, head, rest = sweep_end(far, far_rest, base)
    (x,) = run(
        last_head_kernel,
        [(FULL, f32)],
        [(kept, "v"), (far, "v"), (base, "v"), (ratio, "v")],
        cost=HEAD_COST,
    )
    (x,) = run(
        last_rest_kernel,
        [(FULL, f32)],
        [(kept, "v"), (far_rest, "v"), (ratio, "v"), (x, "v")],
        [pltpu.VMEM(REST, f32), pltpu.SemaphoreType.DMA((TILE_ROWS,))],
        REST_COST,
        hbm_outs=(0,),
    )
    return x


def solution(mesh):
    in_specs = (
        P("rows", "rhs"),
        P("rows", None, None, None),
        P("rows", None),
        P("rows"),
        P("rows"),
        P(("rhs", "rows"), None, None, None),
        P(("rhs", "rows")),
    )
    return jax.shard_map(
        shards, mesh=mesh, in_specs=in_specs, out_specs=P("rows", "rhs"), check_vma=False
    )
```

```python
import functools

import jax
import jax.numpy as jnp
from jax import lax
from jax.experimental import pallas as pl
from jax.experimental.pallas import tpu as pltpu
from jax.sharding import PartitionSpec as P

CYCLES = 2
CHEB = 3
RELAX = 0.7
THETA = 1.0
DELTA = 0.6

B = 128
ROWS = 16
GROUP = 4
TILE = GROUP * B
TILE_ROWS = ROWS // GROUP
SLOTS = 36
FIELD = ROWS * B
TAIL = 16
QROWS = 4 * B
PIECE = 3 * TILE

f32 = jnp.float32
bf16 = jnp.bfloat16
VMEM_SPEC = pl.BlockSpec(memory_space=pltpu.VMEM)
SMEM_SPEC = pl.BlockSpec(memory_space=pltpu.SMEM)
ANY_SPEC = pl.BlockSpec(memory_space=pl.ANY)
LIMIT = 12 * 1024 * 1024


def resident(x):
    return pltpu.with_memory_space_constraint(x, pltpu.VMEM)


def core_of():
    return lax.rem(lax.axis_index("rows"), 2)


def column(row):
    return jnp.transpose(jnp.broadcast_to(row, (B, B)))


def places(columns_ref, out_ref):
    row = lax.broadcasted_iota(jnp.int32, (ROWS, 2 * ROWS), 0)
    first = lax.axis_index("rows") * ROWS - ROWS
    offset = jnp.bitwise_and(columns_ref[...] - first - row + 512, 511)
    offset = jnp.minimum(offset, 2 * ROWS)
    start = row * SLOTS + jnp.bitwise_and(row, GROUP - 1)
    missing = ROWS * (2 * ROWS + 1) - jnp.sum(offset, axis=1, keepdims=True)
    missing = jnp.clip(missing, 0, 2 * ROWS) + start[:, 0:1]
    out_ref[:, 0 : 2 * ROWS] = start + offset
    out_ref[:, 2 * ROWS : B] = jnp.broadcast_to(missing, (ROWS, B - 2 * ROWS))


def start_kernel(
    right_ref, diag_ref, group_ref, coarse_ref, coarse_diag_ref, columns_ref,
    first_ref, sent_ref, head_ref, rest_ref, ratio_ref, diag_out_ref, packed_ref, places_ref,
    right_s, diag_s, group_s, coarse_s, coarse_diag_s, columns_s, sems,
):
    chunks = [
        pltpu.make_async_copy(
            right_ref.at[pl.ds(g * TILE, TILE), :], right_s.at[pl.ds(g * TILE, TILE), :], sems.at[g]
        )
        for g in range(TILE_ROWS)
    ]
    diag_copy = pltpu.make_async_copy(diag_ref, diag_s, sems.at[TILE_ROWS])
    group_copy = pltpu.make_async_copy(group_ref, group_s, sems.at[TILE_ROWS + 1])
    coarse_copy = pltpu.make_async_copy(coarse_ref, coarse_s, sems.at[TILE_ROWS + 2])
    coarse_diag_copy = pltpu.make_async_copy(coarse_diag_ref, coarse_diag_s, sems.at[TILE_ROWS + 3])
    columns_copy = pltpu.make_async_copy(columns_ref, columns_s, sems.at[TILE_ROWS + 4])
    columns_copy.start()
    coarse_diag_copy.start()
    coarse_copy.start()
    diag_copy.start()
    for chunk in chunks:
        chunk.start()
    group_copy.start()
    columns_copy.wait()
    places(columns_s, places_ref)
    coarse_diag_copy.wait()
    coarse_copy.wait()
    pack(coarse_s, coarse_diag_s, packed_ref)
    diag_copy.wait()
    for g in range(TILE_ROWS):
        chunks[g].wait()
        for r in range(g * GROUP, (g + 1) * GROUP):
            rows = pl.ds(r * B, B)
            diag = column(diag_s[r : r + 1, :])
            ratio = RELAX / diag
            value = ratio * right_s[rows, :]
            diag_out_ref[rows, :] = diag
            ratio_ref[rows, :] = ratio
            first_ref[rows, :] = value
            sent_ref[rows, :] = value.astype(bf16)
    even = core_of() == 0
    head = pl.multiple_of(jnp.where(even, 0, TILE), TILE)
    rest = pl.multiple_of(jnp.where(even, PIECE, 0), TILE)
    head_ref[pl.ds(0, PIECE), :] = sent_ref[pl.ds(head, PIECE), :]
    rest_ref[...] = sent_ref[pl.ds(rest, TILE), :]
    group_copy.wait()
    size = lax.axis_size("rows")
    index = lax.broadcasted_iota(jnp.int32, (TAIL, B), 0)
    tail = jnp.zeros((TAIL, B), f32)
    for r in range(ROWS):
        tail = jnp.where(index == r, lax.div(group_s[r], size).astype(f32), tail)
    sent_ref[pl.ds(FIELD, TAIL), :] = tail.astype(bf16)
    head_ref[pl.ds(PIECE, TAIL), :] = tail.astype(bf16)


def pack(blocks_ref, diag_ref, out_ref):
    inverse = 1.0 / diag_ref[...]
    scale = column(inverse)
    for d in range(3):
        out_ref[pl.ds(d * B, B), :] = (scale * blocks_ref[0, d]).astype(bf16)
    high = inverse.astype(bf16).astype(f32)
    low = inverse - high
    index = lax.broadcasted_iota(jnp.int32, (TAIL, B), 0)
    out_ref[pl.ds(3 * B, TAIL), :] = jnp.where(index == 0, high, low).astype(bf16)


def sort_kernel(p0_ref, p1_ref, p2_ref, p3_ref, after_ref, ops_ref, scale_ref):
    me = lax.axis_index("rhs")
    for k, ref in enumerate((p0_ref, p1_ref, p2_ref, p3_ref)):
        q = jnp.bitwise_and(me - k + 4, 3)
        for d in range(3):
            ops_ref[q * 3 + d] = ref[pl.ds(d * B, B), :]
        tail = ref[pl.ds(3 * B, TAIL), :].astype(f32)
        scale_ref[pl.ds(q * B, B), :] = column(tail[0:1, :] + tail[1:2, :])


def tile_product(kept_ref, group, slot, count, field):
    lhs = jnp.concatenate(
        [
            jnp.concatenate(
                [kept_ref[(group * GROUP + a) * SLOTS + slot + b] for b in range(GROUP * count)],
                axis=1,
            )
            for a in range(GROUP)
        ],
        axis=0,
    )
    return jnp.dot(lhs, field, preferred_element_type=f32)


def rows_of(group):
    return pl.ds(pl.multiple_of(group * TILE, TILE), TILE)


def field_at(ref, tile, count):
    return ref[pl.ds(pl.multiple_of(tile * TILE, TILE), count * TILE), :]


def group_of(upper, m):
    return jnp.where(upper, m, TILE_ROWS - 1 - m)


def side_slot(upper, m, j):
    return jnp.where(upper, GROUP * (2 * TILE_ROWS - m + j), GROUP * j)


def near_products(kept_ref, own_ref, near_ref, first, second, straight=False, ready=None):
    @pl.loop(0, TILE_ROWS)
    def _(group):
        if ready is not None:
            ready(group)
        part = tile_product(
            kept_ref, group, GROUP * (TILE_ROWS - group), TILE_ROWS, own_ref[pl.ds(0, FIELD), :]
        )
        first(rows_of(group), part)

    upper = core_of() == 0

    def side(m, j, count):
        group = group_of(upper, m)
        field = field_at(near_ref, jnp.where(upper, j, TILE_ROWS - 1 - m + j), count)
        second(rows_of(group), tile_product(kept_ref, group, side_slot(upper, m, j), count, field))

    if straight:
        for m in range(TILE_ROWS):
            side(m, 0, m + 1)
        return

    @pl.loop(0, 4)
    def _(p):
        side(jnp.minimum(p + 1, 3), jnp.where(p == 3, 2, 0), 2)

    @pl.loop(0, 2)
    def _(p):
        side(2 * p, 2 * p, 1)


def far_products(kept_ref, far_ref, emit):
    upper = core_of() == 1
    for m in range(TILE_ROWS):
        group = group_of(upper, m)
        field = field_at(far_ref, jnp.where(upper, 0, TILE_ROWS - 1 - m), m + 1)
        emit(m, rows_of(group), tile_product(kept_ref, group, side_slot(upper, m, 0), m + 1, field))


def head_products(kept_ref, head_ref, emit):
    upper = core_of() == 1
    for m in range(TILE_ROWS - 1):
        group = group_of(upper, m)
        field = field_at(head_ref, jnp.where(upper, 0, TILE_ROWS - 2 - m), m + 1)
        emit(m, rows_of(group), tile_product(kept_ref, group, side_slot(upper, m, 0), m + 1, field))
    m = TILE_ROWS - 1
    group = group_of(upper, m)
    slot = jnp.where(upper, side_slot(True, m, 0), side_slot(False, m, 1))
    emit(m, rows_of(group), tile_product(kept_ref, group, slot, m, field_at(head_ref, 0, m)))


def rest_product(kept_ref, rest_ref):
    upper = core_of() == 1
    m = TILE_ROWS - 1
    group = group_of(upper, m)
    slot = jnp.where(upper, side_slot(True, m, m), side_slot(False, m, 0))
    return rows_of(group), tile_product(kept_ref, group, slot, 1, rest_ref[...])


def send(m, rows, value, sent_ref, head_ref, rest_ref):
    value = value.astype(bf16)
    sent_ref[rows, :] = value
    if m == 0:
        rest_ref[...] = value
    else:
        at = jnp.where(core_of() == 1, m - 1, TILE_ROWS - 1 - m)
        head_ref[rows_of(at), :] = value


def sweep_near(
    kept_ref, own_ref, near_ref, x_ref, first_ref, ratio_ref, base_ref, straight=False, ready=None
):
    def first(rows, part):
        base_ref[rows, :] = (1.0 - RELAX) * x_ref[rows, :] + first_ref[rows, :] - ratio_ref[rows, :] * part

    def second(rows, part):
        base_ref[rows, :] -= ratio_ref[rows, :] * part

    near_products(kept_ref, own_ref, near_ref, first, second, straight, ready)


def sweep_near_kernel(kept_ref, own_ref, near_ref, x_ref, first_ref, ratio_ref, base_ref):
    sweep_near(kept_ref, own_ref, near_ref, x_ref, first_ref, ratio_ref, base_ref)


def load_near_kernel(
    places_ref, blocks_ref, own_ref, near_ref, first_ref, ratio_ref, kept_ref, base_ref, sems
):
    empty = jnp.zeros((B, B), bf16)

    @pl.loop(0, ROWS)
    def _(r):
        sem = sems.at[lax.div(r, GROUP)]
        for k in range(2 * ROWS):
            pltpu.make_async_copy(blocks_ref.at[r, k], kept_ref.at[places_ref[r, k]], sem).start()

    for r in range(ROWS):
        lead = r % GROUP
        kept_ref[places_ref[r, 2 * ROWS]] = empty
        for pad in range(GROUP - 1):
            kept_ref[r * SLOTS + (pad if pad < lead else 2 * ROWS + 1 + pad)] = empty

    def ready(group):
        for a in range(GROUP):
            r = group * GROUP + a
            pltpu.make_async_copy(
                blocks_ref.at[r], kept_ref.at[pl.ds(r * 2 * ROWS, 2 * ROWS)], sems.at[group]
            ).wait()

    sweep_near(
        kept_ref, own_ref, near_ref, first_ref, first_ref, ratio_ref, base_ref, True, ready
    )


def sweep_head_kernel(kept_ref, far_ref, base_ref, ratio_ref, x_ref, sent_ref, head_ref, rest_ref):
    def emit(m, rows, part):
        value = base_ref[rows, :] - ratio_ref[rows, :] * part
        x_ref[rows, :] = value
        if m < TILE_ROWS - 1:
            send(m, rows, value, sent_ref, head_ref, rest_ref)

    head_products(kept_ref, far_ref, emit)


def sweep_rest_kernel(
    kept_ref, far_ref, ratio_ref, x_in, sent_in, head_in, x_ref, sent_ref, head_ref
):
    rows, part = rest_product(kept_ref, far_ref)
    value = x_in[rows, :] - ratio_ref[rows, :] * part
    x_ref[rows, :] = value
    send(TILE_ROWS - 1, rows, value, sent_ref, head_ref, None)


def last_head_kernel(kept_ref, far_ref, base_ref, ratio_ref, x_ref):
    def emit(m, rows, part):
        x_ref[rows, :] = base_ref[rows, :] - ratio_ref[rows, :] * part

    head_products(kept_ref, far_ref, emit)


def last_rest_kernel(kept_ref, far_ref, ratio_ref, x_in, x_ref, x_s, sems):
    upper = core_of() == 1
    copies = []
    for m in range(TILE_ROWS - 1):
        done = rows_of(group_of(upper, m))
        copies.append(pltpu.make_async_copy(x_in.at[done, :], x_ref.at[done, :], sems.at[m]))
        copies[m].start()
    rows, part = rest_product(kept_ref, far_ref)
    x_s[...] = x_in[rows, :] - ratio_ref[rows, :] * part
    copies.append(pltpu.make_async_copy(x_s, x_ref.at[rows, :], sems.at[TILE_ROWS - 1]))
    copies[-1].start()
    for copy in copies:
        copy.wait()


def residual_near_kernel(
    straight, kept_ref, own_ref, near_ref, x_ref, right_ref, diag_ref, base_ref
):
    def first(rows, part):
        base_ref[rows, :] = right_ref[rows, :] - diag_ref[rows, :] * x_ref[rows, :] - part

    def second(rows, part):
        base_ref[rows, :] -= part

    near_products(kept_ref, own_ref, near_ref, first, second, straight)


def residual_head_kernel(kept_ref, group_ref, far_ref, base_ref, res_ref, side_ref):
    side_ref[...] = jnp.zeros((QROWS, B), f32)
    upper = core_of() == 1

    def emit(m, rows, part):
        value = base_ref[rows, :] - part
        res_ref[rows, :] = value
        if m < TILE_ROWS - 1:
            for a in range(GROUP):
                group = lax.div(group_ref[group_of(upper, m) * GROUP + a], lax.axis_size("rows"))
                side_ref[pl.ds(pl.multiple_of(group * B, B), B), :] += value[a * B : (a + 1) * B, :]

    head_products(kept_ref, far_ref, emit)


def residual_far_kernel(
    kept_ref, group_ref, far_ref, base_ref, scale_ref, res_ref, side_ref, sent_ref
):
    upper = core_of() == 1
    side_ref[...] = jnp.zeros((QROWS, B), f32)

    def emit(m, rows, part):
        value = base_ref[rows, :] - part
        res_ref[rows, :] = value
        for a in range(GROUP):
            group = lax.div(group_ref[group_of(upper, m) * GROUP + a], lax.axis_size("rows"))
            side_ref[pl.ds(pl.multiple_of(group * B, B), B), :] += value[a * B : (a + 1) * B, :]

    far_products(kept_ref, far_ref, emit)
    value = scale_ref[...] * side_ref[...]
    side_ref[...] = value
    sent_ref[...] = value.astype(bf16)


def residual_rest_kernel(
    kept_ref, tail_ref, far_ref, scale_ref, res_in, side_in, res_ref, side_ref, sent_ref
):
    upper = (core_of() == 1).astype(f32)
    tail = tail_ref[pl.ds(FIELD, TAIL), :].astype(f32)
    rows, part = rest_product(kept_ref, far_ref)
    value = res_in[rows, :] - part
    res_ref[rows, :] = value
    for q in range(4):
        place = pl.ds(q * B, B)
        total = side_in[place, :]
        for a in range(GROUP):
            at = TAIL - GROUP + a
            group = upper * tail[at : at + 1, :] + (1.0 - upper) * tail[a : a + 1, :]
            total = total + jnp.where(group == q, 1.0, 0.0) * value[a * B : (a + 1) * B, :]
        total = scale_ref[place, :] * total
        side_ref[place, :] = total
        sent_ref[place, :] = total.astype(bf16)


def spread(coarse_ref, tail_ref, start, out_ref):
    tail = tail_ref[pl.ds(start, TAIL), :].astype(f32)
    parts = [coarse_ref[pl.ds(q * B, B), :].astype(f32) for q in range(4)]
    for r in range(ROWS):
        group = tail[r : r + 1, :]
        value = jnp.where(group < 0.5, parts[0], parts[1])
        value = jnp.where(group < 1.5, value, parts[2])
        value = jnp.where(group < 2.5, value, parts[3])
        out_ref[pl.ds(r * B, B), :] = value.astype(bf16)


def lift_near_kernel(
    kept_ref, group_ref, coarse_ref, near_ref, near_tail_ref, x_ref, res_ref, ratio_ref, base_ref, own_s, near_s
):
    for r in range(ROWS):
        rows = pl.ds(pl.multiple_of(lax.div(group_ref[r], lax.axis_size("rows")) * B, B), B)
        own_s[pl.ds(r * B, B), :] = coarse_ref[rows, :]
    spread(near_ref, near_tail_ref, FIELD, near_s)

    def first(rows, part):
        base_ref[rows, :] = (
            x_ref[rows, :]
            + (1.0 - RELAX) * own_s[rows, :].astype(f32)
            + ratio_ref[rows, :] * (res_ref[rows, :] - part)
        )

    def second(rows, part):
        base_ref[rows, :] -= ratio_ref[rows, :] * part

    near_products(kept_ref, own_s, near_s, first, second)


def lift_far_kernel(
    kept_ref, far_ref, far_tail_ref, base_ref, ratio_ref, x_ref, sent_ref, head_ref, rest_ref, far_s
):
    spread(far_ref, far_tail_ref, PIECE, far_s)

    def emit(m, rows, part):
        value = base_ref[rows, :] - ratio_ref[rows, :] * part
        x_ref[rows, :] = value
        send(m, rows, value, sent_ref, head_ref, rest_ref)

    far_products(kept_ref, far_s, emit)


def coarse_terms(ops_ref, own_ref, near_ref, far_ref, emit):
    i = lax.axis_index("rows")
    last = lax.axis_size("rows") - 1
    near_is_upper = (core_of() == 0).astype(f32)
    step_up = (i == last).astype(jnp.int32)
    step_down = (i == 0).astype(jnp.int32)
    for q in range(4):
        at_up = pl.multiple_of(jnp.minimum(q + step_up, 3) * B, B)
        at_down = pl.multiple_of(jnp.maximum(q - step_down, 0) * B, B)
        keep_up = (q + step_up <= 3).astype(f32)
        keep_down = (q - step_down >= 0).astype(f32)
        upper = near_is_upper * near_ref[pl.ds(at_up, B), :].astype(f32) + (
            1.0 - near_is_upper
        ) * far_ref[pl.ds(at_up, B), :].astype(f32)
        lower = near_is_upper * far_ref[pl.ds(at_down, B), :].astype(f32) + (
            1.0 - near_is_upper
        ) * near_ref[pl.ds(at_down, B), :].astype(f32)
        field = jnp.concatenate(
            [
                (keep_down * lower).astype(bf16),
                own_ref[pl.ds(q * B, B), :],
                (keep_up * upper).astype(bf16),
            ],
            axis=0,
        )
        ops = jnp.concatenate([ops_ref[q * 3 + d] for d in range(3)], axis=1)
        emit(pl.ds(q * B, B), jnp.dot(ops, field, preferred_element_type=f32))


def ratios():
    sigma = THETA / DELTA
    old = 1.0 / sigma
    out = []
    for _ in range(CHEB - 1):
        new = 1.0 / (2.0 * sigma - old)
        out.append((new * old, 2.0 * new / DELTA))
        old = new
    return out


def coarse_first_kernel(
    ops_ref, side_ref, own_ref, near_ref, far_ref, fix_ref, sent_ref, ops_out_ref
):
    keep, gain = ratios()[0]

    def emit(rows, part):
        side = side_ref[rows, :] / THETA
        fix = side + keep * side + gain * (side_ref[rows, :] - side - part)
        fix_ref[rows, :] = fix
        sent_ref[rows, :] = fix.astype(bf16)

    coarse_terms(ops_ref, own_ref, near_ref, far_ref, emit)
    for n in range(12):
        ops_out_ref[pl.ds(n * B, B), :] = ops_ref[n]


def coarse_second_kernel(ops_ref, side_ref, fix_ref, own_ref, near_ref, far_ref, sent_ref):
    keep, gain = ratios()[1]

    def emit(rows, part):
        fix = fix_ref[rows, :]
        update = fix - side_ref[rows, :] / THETA
        fix = fix + keep * update + gain * (side_ref[rows, :] - fix - part)
        sent_ref[rows, :] = fix.astype(bf16)

    coarse_terms(ops_ref, own_ref, near_ref, far_ref, emit)


def join_kernel(own_ref, near_ref, out_ref):
    out_ref[pl.ds(0, QROWS), :] = own_ref[...]
    out_ref[pl.ds(QROWS, QROWS), :] = near_ref[...]


def coarse_wide_kernel(
    ops_ref, near_ops_ref, far_ops_ref, side_ref, own_ref, near_ref, far_ref, beyond_ref, sent_ref,
    near_s, far_s, fix_s,
):
    i = lax.axis_index("rows")
    last = lax.axis_size("rows") - 1
    near_dir = jnp.where(core_of() == 0, 2, 0)
    far_dir = 2 - near_dir
    far_step = (i == last).astype(jnp.int32) - (i == 0).astype(jnp.int32)
    beyond_step = (i == last - 1).astype(jnp.int32) - (i == 1).astype(jnp.int32)
    keep, gain = ratios()[0]
    keep_next, gain_next = ratios()[1]

    def at(q, step):
        return jnp.clip(q + step, 0, 3)

    def inside(q, step):
        return jnp.logical_and(q + step >= 0, q + step <= 3).astype(f32)

    def block(ref, q, step=None, start=0):
        if step is None:
            return ref[pl.ds(start + q * B, B), :]
        value = ref[pl.ds(pl.multiple_of(start + at(q, step) * B, B), B), :]
        return (inside(q, step) * value.astype(f32)).astype(bf16)

    def product(ops, fields):
        return jnp.dot(
            jnp.concatenate(ops, axis=1),
            jnp.concatenate(fields, axis=0),
            preferred_element_type=f32,
        )

    for q in range(4):
        rows = pl.ds(q * B, B)
        own, near, far = block(own_ref, q), block(near_ref, q), block(far_ref, q, far_step)
        part = product(
            [ops_ref[q * 3 + far_dir], ops_ref[q * 3 + 1], ops_ref[q * 3 + near_dir]],
            [far, own, near],
        )
        side = side_ref[rows, :] / THETA
        fix_s[rows, :] = side + keep * side + gain * (side_ref[rows, :] - side - part)
        ops = [near_ops_ref[pl.ds((q * 3 + d) * B, B), :] for d in range(3)]
        lower_is_own = (near_dir == 2).astype(f32)
        beyond = block(beyond_ref, q, beyond_step).astype(f32)
        own_f = own.astype(f32)
        low = (lower_is_own * own_f + (1.0 - lower_is_own) * beyond).astype(bf16)
        high = (lower_is_own * beyond + (1.0 - lower_is_own) * own_f).astype(bf16)
        part = product(ops, [low, near, high])
        value = near.astype(f32)
        side = value / THETA
        near_s[rows, :] = (side + keep * side + gain * (value - side - part)).astype(bf16)
        first = pl.multiple_of(at(q, far_step) * 3 * B, B)
        ops = [far_ops_ref[pl.ds(pl.multiple_of(first + d * B, B), B), :] for d in range(3)]
        outer = block(far_ref, q, far_step, QROWS).astype(f32)
        low = (lower_is_own * outer + (1.0 - lower_is_own) * own_f).astype(bf16)
        high = (lower_is_own * own_f + (1.0 - lower_is_own) * outer).astype(bf16)
        part = product(ops, [low, far, high])
        value = far.astype(f32)
        side = value / THETA
        fix = side + keep * side + gain * (value - side - part)
        far_s[rows, :] = (inside(q, far_step) * fix).astype(bf16)
    for q in range(4):
        rows = pl.ds(q * B, B)
        fix = fix_s[rows, :]
        part = product(
            [ops_ref[q * 3 + far_dir], ops_ref[q * 3 + 1], ops_ref[q * 3 + near_dir]],
            [far_s[rows, :], fix.astype(bf16), near_s[rows, :]],
        )
        update = fix - side_ref[rows, :] / THETA
        fix = fix + keep_next * update + gain_next * (side_ref[rows, :] - fix - part)
        sent_ref[rows, :] = fix.astype(bf16)


def run(kernel, outs, args, scratch=(), cost=(0, 0), hbm_outs=(), alias={}):
    specs, values = [], []
    for value, space in args:
        if space == "v":
            specs.append(VMEM_SPEC)
            values.append(resident(value))
        elif space == "b":
            specs.append(VMEM_SPEC)
            values.append(value)
        elif space == "s":
            specs.append(SMEM_SPEC)
            values.append(value)
        elif space == "a":
            specs.append(ANY_SPEC)
            values.append(value)
        else:
            specs.append(ANY_SPEC)
            values.append(pltpu.with_memory_space_constraint(value, pltpu.HBM))
    return pl.pallas_call(
        kernel,
        out_shape=[
            jax.ShapeDtypeStruct(shape, dtype) if n in hbm_outs else pltpu.VMEM(shape, dtype)
            for n, (shape, dtype) in enumerate(outs)
        ],
        in_specs=specs,
        out_specs=[ANY_SPEC if n in hbm_outs else VMEM_SPEC for n in range(len(outs))],
        input_output_aliases=alias,
        scratch_shapes=list(scratch),
        cost_estimate=pl.CostEstimate(flops=cost[0], bytes_accessed=cost[1], transcendentals=0),
        compiler_params=pltpu.CompilerParams(vmem_limit_bytes=LIMIT),
    )(*values)


def swap_near(x, size):
    return lax.ppermute(x, "rows", [(i, i ^ 1) for i in range(size)])


def swap_far(x, size):
    pairs = [(i, (i - 1) % size if i % 2 == 0 else (i + 1) % size) for i in range(size)]
    return lax.ppermute(x, "rows", pairs)


FULL = (FIELD, B)
HEAD = (PIECE, B)
REST = (TILE, B)
SIDE = (QROWS, B)
TILE_FLOPS = 2 * TILE * TILE * B
NEAR_COST = (26 * TILE_FLOPS, 8_000_000)
HEAD_COST = (9 * TILE_FLOPS, 3_000_000)
REST_COST = (TILE_FLOPS, 1_000_000)
FIELDS = [(FULL, f32), (FULL, bf16), (HEAD, bf16), (REST, bf16)]


def shards(right_side, fine_blocks, fine_columns, fine_diag, aggregate, coarse_blocks, coarse_diag):
    size = lax.axis_size("rows")

    first, sent, head, rest, ratio, diag, packed, places_of = run(
        start_kernel,
        [
            (FULL, f32), ((FIELD + TAIL, B), bf16), ((PIECE + TAIL, B), bf16), (REST, bf16),
            (FULL, f32), (FULL, f32), ((3 * B + TAIL, B), bf16),
            ((ROWS, B), jnp.int32),
        ],
        [
            (right_side, "h"), (fine_diag.reshape(ROWS, B), "h"), (aggregate, "h"),
            (coarse_blocks, "h"), (coarse_diag.reshape(1, B), "h"),
            (fine_columns, "h"),
        ],
        [
            pltpu.VMEM(FULL, f32),
            pltpu.VMEM((ROWS, B), f32),
            pltpu.SMEM((ROWS,), jnp.int32),
            pltpu.VMEM((1, 3, B, B), f32),
            pltpu.VMEM((1, B), f32),
            pltpu.VMEM((ROWS, 2 * ROWS), jnp.int32),
            pltpu.SemaphoreType.DMA((TILE_ROWS + 5,)),
        ],
    )

    def swap_fields(sent, head, rest):
        return swap_far(head, size), swap_far(rest, size), swap_near(sent, size)

    def swap_sides(sent):
        return swap_far(sent, size), swap_near(sent, size)

    pieces = [packed] + [
        lax.ppermute(packed, "rhs", [(i, (i + k) % 4) for i in range(4)]) for k in range(1, 4)
    ]
    far, far_rest, near = swap_fields(sent, head, rest)
    own_tail, near_tail, far_tail = sent, near, far
    kept, base = run(
        load_near_kernel,
        [((ROWS * SLOTS, B, B), bf16), (FULL, f32)],
        [
            (places_of, "s"), (fine_blocks, "h"), (sent, "v"), (near, "v"), (first, "v"),
            (ratio, "v"),
        ],
        [pltpu.SemaphoreType.DMA((TILE_ROWS,))],
        (NEAR_COST[0], 28_000_000),
    )

    def sweep_start(x, sent, near):
        return run(
            sweep_near_kernel,
            [(FULL, f32)],
            [(kept, "v"), (sent, "v"), (near, "v"), (x, "v"), (first, "v"), (ratio, "v")],
            cost=NEAR_COST,
        )[0]

    def sweep_end(far, far_rest, base):
        x, sent, head, rest = run(
            sweep_head_kernel,
            FIELDS,
            [(kept, "v"), (far, "v"), (base, "v"), (ratio, "v")],
            cost=HEAD_COST,
        )
        x, sent, head = run(
            sweep_rest_kernel,
            FIELDS[:3],
            [(kept, "v"), (far_rest, "v"), (ratio, "v"), (x, "v"), (sent, "v"), (head, "v")],
            cost=REST_COST,
            alias={3: 0, 4: 1, 5: 2},
        )
        return x, sent, head, rest

    x = first
    for turn in range(CYCLES):
        for _ in range(2 * (turn > 0)):
            far, far_rest, near = swap_fields(sent, head, rest)
            base = sweep_start(x, sent, near)
            x, sent, head, rest = sweep_end(far, far_rest, base)
        if turn == 0:
            x, sent, head, rest = sweep_end(far, far_rest, base)
        if turn == 0:
            far, near = swap_sides(sent)
        else:
            far, far_rest, near = swap_fields(sent, head, rest)
        (base,) = run(
            functools.partial(residual_near_kernel, turn == 0),
            [(FULL, f32)],
            [(kept, "v"), (sent, "v"), (near, "v"), (x, "v"), (right_side, "b"), (diag, "v")],
            cost=NEAR_COST,
        )
        if turn == 0:
            ops, scale = run(
                sort_kernel,
                [((12, B, B), bf16), (SIDE, f32)],
                [(p, "v") for p in pieces] + [(base, "v")],
            )
            res, side, sent = run(
                residual_far_kernel,
                [(FULL, f32), (SIDE, f32), (SIDE, bf16)],
                [(kept, "v"), (aggregate, "s"), (far, "v"), (base, "v"), (scale, "v")],
                cost=HEAD_COST,
            )
        else:
            res, side = run(
                residual_head_kernel,
                [(FULL, f32), (SIDE, f32)],
                [(kept, "v"), (aggregate, "s"), (far, "v"), (base, "v")],
                cost=HEAD_COST,
            )
            res, side, sent = run(
                residual_rest_kernel,
                [(FULL, f32), (SIDE, f32), (SIDE, bf16)],
                [
                    (kept, "v"), (own_tail, "v"), (far_rest, "v"), (scale, "v"), (res, "v"),
                    (side, "v"),
                ],
                cost=REST_COST,
                alias={4: 0, 5: 1},
            )
        if turn == 0:
            far, near = swap_sides(sent)
            fix, sent, ops_sent = run(
                coarse_first_kernel,
                [(SIDE, f32), (SIDE, bf16), ((12 * B, B), bf16)],
                [(ops, "v"), (side, "v"), (sent, "v"), (near, "v"), (far, "v")],
            )
            far, near = swap_sides(sent)
            far_ops, near_ops = swap_sides(ops_sent)
            (sent,) = run(
                coarse_second_kernel,
                [(SIDE, bf16)],
                [(ops, "v"), (side, "v"), (fix, "v"), (sent, "v"), (near, "v"), (far, "v")],
            )
        else:
            near = swap_near(sent, size)
            (pair,) = run(join_kernel, [((2 * QROWS, B), bf16)], [(sent, "v"), (near, "v")])
            far = swap_far(pair, size)
            beyond = swap_near(far, size)
            (sent,) = run(
                coarse_wide_kernel,
                [(SIDE, bf16)],
                [
                    (ops, "v"), (near_ops, "v"), (far_ops, "v"), (side, "v"), (sent, "v"),
                    (near, "v"), (far, "v"), (beyond, "v"),
                ],
                [pltpu.VMEM(SIDE, bf16), pltpu.VMEM(SIDE, bf16), pltpu.VMEM(SIDE, f32)],
            )
        far, near = swap_sides(sent)
        (base,) = run(
            lift_near_kernel,
            [(FULL, f32)],
            [
                (kept, "v"), (aggregate, "s"), (sent, "v"), (near, "v"), (near_tail, "v"),
                (x, "v"), (res, "v"), (ratio, "v"),
            ],
            [pltpu.VMEM(FULL, bf16), pltpu.VMEM(FULL, bf16)],
            NEAR_COST,
        )
        x, sent, head, rest = run(
            lift_far_kernel,
            FIELDS,
            [(kept, "v"), (far, "v"), (far_tail, "v"), (base, "v"), (ratio, "v")],
            [pltpu.VMEM(FULL, bf16)],
            (10 * TILE_FLOPS, 3_000_000),
        )
        far, far_rest, near = swap_fields(sent, head, rest)
        base = sweep_start(x, sent, near)
        if turn < CYCLES - 1:
            x, sent, head, rest = sweep_end(far, far_rest, base)
    (x,) = run(
        last_head_kernel,
        [(FULL, f32)],
        [(kept, "v"), (far, "v"), (base, "v"), (ratio, "v")],
        cost=HEAD_COST,
    )
    (x,) = run(
        last_rest_kernel,
        [(FULL, f32)],
        [(kept, "v"), (far_rest, "v"), (ratio, "v"), (x, "v")],
        [pltpu.VMEM(REST, f32), pltpu.SemaphoreType.DMA((TILE_ROWS,))],
        REST_COST,
        hbm_outs=(0,),
    )
    return x


def solution(mesh):
    in_specs = (
        P("rows", "rhs"),
        P("rows", None, None, None),
        P("rows", None),
        P("rows"),
        P("rows"),
        P(("rhs", "rows"), None, None, None),
        P(("rhs", "rows")),
    )
    return jax.shard_map(
        shards, mesh=mesh, in_specs=in_specs, out_specs=P("rows", "rhs"), check_vma=False
    )
```

```python
import functools

import jax
import jax.numpy as jnp
from jax import lax
from jax.experimental import pallas as pl
from jax.experimental.pallas import tpu as pltpu
from jax.sharding import PartitionSpec as P

CYCLES = 2
CHEB = 3
RELAX = 0.7
THETA = 1.0
DELTA = 0.6

B = 128
ROWS = 16
GROUP = 4
TILE = GROUP * B
TILE_ROWS = ROWS // GROUP
SLOTS = 36
FIELD = ROWS * B
TAIL = 16
QROWS = 4 * B
PIECE = 3 * TILE

f32 = jnp.float32
bf16 = jnp.bfloat16
VMEM_SPEC = pl.BlockSpec(memory_space=pltpu.VMEM)
SMEM_SPEC = pl.BlockSpec(memory_space=pltpu.SMEM)
ANY_SPEC = pl.BlockSpec(memory_space=pl.ANY)
LIMIT = 12 * 1024 * 1024


def resident(x):
    return pltpu.with_memory_space_constraint(x, pltpu.VMEM)


def core_of():
    return lax.rem(lax.axis_index("rows"), 2)


def column(row):
    return jnp.transpose(jnp.broadcast_to(row, (B, B)))


def places(columns_ref, out_ref):
    row = lax.broadcasted_iota(jnp.int32, (ROWS, 2 * ROWS), 0)
    first = lax.axis_index("rows") * ROWS - ROWS
    offset = jnp.bitwise_and(columns_ref[...] - first - row + 512, 511)
    offset = jnp.minimum(offset, 2 * ROWS)
    start = row * SLOTS + jnp.bitwise_and(row, GROUP - 1)
    missing = ROWS * (2 * ROWS + 1) - jnp.sum(offset, axis=1, keepdims=True)
    missing = jnp.clip(missing, 0, 2 * ROWS) + start[:, 0:1]
    out_ref[:, 0 : 2 * ROWS] = start + offset
    out_ref[:, 2 * ROWS : B] = jnp.broadcast_to(missing, (ROWS, B - 2 * ROWS))


def start_kernel(
    right_ref, diag_ref, group_ref, coarse_ref, coarse_diag_ref, columns_ref,
    first_ref, sent_ref, ratio_ref, diag_out_ref, packed_ref, places_ref,
    right_s, diag_s, group_s, coarse_s, coarse_diag_s, columns_s, sems,
):
    chunks = [
        pltpu.make_async_copy(
            right_ref.at[pl.ds(g * TILE, TILE), :], right_s.at[pl.ds(g * TILE, TILE), :], sems.at[g]
        )
        for g in range(TILE_ROWS)
    ]
    diag_copy = pltpu.make_async_copy(diag_ref, diag_s, sems.at[TILE_ROWS])
    group_copy = pltpu.make_async_copy(group_ref, group_s, sems.at[TILE_ROWS + 1])
    coarse_copy = pltpu.make_async_copy(coarse_ref, coarse_s, sems.at[TILE_ROWS + 2])
    coarse_diag_copy = pltpu.make_async_copy(coarse_diag_ref, coarse_diag_s, sems.at[TILE_ROWS + 3])
    columns_copy = pltpu.make_async_copy(columns_ref, columns_s, sems.at[TILE_ROWS + 4])
    columns_copy.start()
    coarse_diag_copy.start()
    coarse_copy.start()
    diag_copy.start()
    for chunk in chunks:
        chunk.start()
    group_copy.start()
    columns_copy.wait()
    places(columns_s, places_ref)
    coarse_diag_copy.wait()
    coarse_copy.wait()
    pack(coarse_s, coarse_diag_s, packed_ref)
    diag_copy.wait()
    for g in range(TILE_ROWS):
        chunks[g].wait()
        for r in range(g * GROUP, (g + 1) * GROUP):
            rows = pl.ds(r * B, B)
            diag = column(diag_s[r : r + 1, :])
            ratio = RELAX / diag
            value = ratio * right_s[rows, :]
            diag_out_ref[rows, :] = diag
            ratio_ref[rows, :] = ratio
            first_ref[rows, :] = value
            sent_ref[rows, :] = value.astype(bf16)
    group_copy.wait()
    size = lax.axis_size("rows")
    index = lax.broadcasted_iota(jnp.int32, (TAIL, B), 0)
    tail = jnp.zeros((TAIL, B), f32)
    for r in range(ROWS):
        tail = jnp.where(index == r, lax.div(group_s[r], size).astype(f32), tail)
    sent_ref[pl.ds(FIELD, TAIL), :] = tail.astype(bf16)


def pack(blocks_ref, diag_ref, out_ref):
    inverse = 1.0 / diag_ref[...]
    scale = column(inverse)
    for d in range(3):
        out_ref[pl.ds(d * B, B), :] = (scale * blocks_ref[0, d]).astype(bf16)
    high = inverse.astype(bf16).astype(f32)
    low = inverse - high
    index = lax.broadcasted_iota(jnp.int32, (TAIL, B), 0)
    out_ref[pl.ds(3 * B, TAIL), :] = jnp.where(index == 0, high, low).astype(bf16)


def sort_kernel(p0_ref, p1_ref, p2_ref, p3_ref, after_ref, ops_ref, scale_ref):
    me = lax.axis_index("rhs")
    for k, ref in enumerate((p0_ref, p1_ref, p2_ref, p3_ref)):
        q = jnp.bitwise_and(me - k + 4, 3)
        for d in range(3):
            ops_ref[q * 3 + d] = ref[pl.ds(d * B, B), :]
        tail = ref[pl.ds(3 * B, TAIL), :].astype(f32)
        scale_ref[pl.ds(q * B, B), :] = column(tail[0:1, :] + tail[1:2, :])


def tile_product(kept_ref, group, slot, count, field):
    lhs = jnp.concatenate(
        [
            jnp.concatenate(
                [kept_ref[(group * GROUP + a) * SLOTS + slot + b] for b in range(GROUP * count)],
                axis=1,
            )
            for a in range(GROUP)
        ],
        axis=0,
    )
    return jnp.dot(lhs, field, preferred_element_type=f32)


def rows_of(group):
    return pl.ds(pl.multiple_of(group * TILE, TILE), TILE)


def field_at(ref, tile, count):
    return ref[pl.ds(pl.multiple_of(tile * TILE, TILE), count * TILE), :]


def group_of(upper, m):
    return jnp.where(upper, m, TILE_ROWS - 1 - m)


def side_slot(upper, m, j):
    return jnp.where(upper, GROUP * (2 * TILE_ROWS - m + j), GROUP * j)


def near_products(kept_ref, own_ref, near_ref, first, second, straight=False, ready=None):
    @pl.loop(0, TILE_ROWS)
    def _(group):
        if ready is not None:
            ready(group)
        part = tile_product(
            kept_ref, group, GROUP * (TILE_ROWS - group), TILE_ROWS, own_ref[pl.ds(0, FIELD), :]
        )
        first(rows_of(group), part)

    upper = core_of() == 0

    def side(m, j, count):
        group = group_of(upper, m)
        field = field_at(near_ref, jnp.where(upper, j, TILE_ROWS - 1 - m + j), count)
        second(rows_of(group), tile_product(kept_ref, group, side_slot(upper, m, j), count, field))

    if straight:
        for m in range(TILE_ROWS):
            side(m, 0, m + 1)
        return

    @pl.loop(0, 4)
    def _(p):
        side(jnp.minimum(p + 1, 3), jnp.where(p == 3, 2, 0), 2)

    @pl.loop(0, 2)
    def _(p):
        side(2 * p, 2 * p, 1)


def far_products(kept_ref, far_ref, emit):
    upper = core_of() == 1
    for m in range(TILE_ROWS):
        group = group_of(upper, m)
        field = field_at(far_ref, jnp.where(upper, 0, TILE_ROWS - 1 - m), m + 1)
        emit(m, rows_of(group), tile_product(kept_ref, group, side_slot(upper, m, 0), m + 1, field))


def head_products(kept_ref, head_ref, emit):
    upper = core_of() == 1
    for m in range(TILE_ROWS - 1):
        group = group_of(upper, m)
        field = field_at(head_ref, jnp.where(upper, 0, TILE_ROWS - 2 - m), m + 1)
        emit(m, rows_of(group), tile_product(kept_ref, group, side_slot(upper, m, 0), m + 1, field))
    m = TILE_ROWS - 1
    group = group_of(upper, m)
    slot = jnp.where(upper, side_slot(True, m, 0), side_slot(False, m, 1))
    emit(m, rows_of(group), tile_product(kept_ref, group, slot, m, field_at(head_ref, 0, m)))


def rest_product(kept_ref, rest_ref):
    upper = core_of() == 1
    m = TILE_ROWS - 1
    group = group_of(upper, m)
    slot = jnp.where(upper, side_slot(True, m, m), side_slot(False, m, 0))
    return rows_of(group), tile_product(kept_ref, group, slot, 1, rest_ref[...])


def send(m, rows, value, sent_ref, head_ref, rest_ref):
    value = value.astype(bf16)
    sent_ref[rows, :] = value
    if m == 0:
        rest_ref[...] = value
    else:
        at = jnp.where(core_of() == 1, m - 1, TILE_ROWS - 1 - m)
        head_ref[rows_of(at), :] = value


def sweep_near(
    kept_ref, own_ref, near_ref, x_ref, first_ref, ratio_ref, base_ref, straight=False, ready=None
):
    def first(rows, part):
        base_ref[rows, :] = (1.0 - RELAX) * x_ref[rows, :] + first_ref[rows, :] - ratio_ref[rows, :] * part

    def second(rows, part):
        base_ref[rows, :] -= ratio_ref[rows, :] * part

    near_products(kept_ref, own_ref, near_ref, first, second, straight, ready)


def sweep_near_kernel(kept_ref, own_ref, near_ref, x_ref, first_ref, ratio_ref, base_ref):
    sweep_near(kept_ref, own_ref, near_ref, x_ref, first_ref, ratio_ref, base_ref)


def load_near_kernel(
    places_ref, blocks_ref, own_ref, near_ref, first_ref, ratio_ref, kept_ref, base_ref, sems
):
    empty = jnp.zeros((B, B), bf16)

    @pl.loop(0, ROWS)
    def _(r):
        sem = sems.at[lax.div(r, GROUP)]
        for k in range(2 * ROWS):
            pltpu.make_async_copy(blocks_ref.at[r, k], kept_ref.at[places_ref[r, k]], sem).start()

    for r in range(ROWS):
        lead = r % GROUP
        kept_ref[places_ref[r, 2 * ROWS]] = empty
        for pad in range(GROUP - 1):
            kept_ref[r * SLOTS + (pad if pad < lead else 2 * ROWS + 1 + pad)] = empty

    def ready(group):
        for a in range(GROUP):
            r = group * GROUP + a
            pltpu.make_async_copy(
                blocks_ref.at[r], kept_ref.at[pl.ds(r * 2 * ROWS, 2 * ROWS)], sems.at[group]
            ).wait()

    sweep_near(
        kept_ref, own_ref, near_ref, first_ref, first_ref, ratio_ref, base_ref, True, ready
    )


def sweep_far_kernel(kept_ref, far_ref, base_ref, ratio_ref, x_ref, sent_ref):
    def emit(m, rows, part):
        value = base_ref[rows, :] - ratio_ref[rows, :] * part
        x_ref[rows, :] = value
        sent_ref[rows, :] = value.astype(bf16)

    far_products(kept_ref, far_ref, emit)


def sweep_head_kernel(kept_ref, far_ref, base_ref, ratio_ref, x_ref, sent_ref, head_ref, rest_ref):
    def emit(m, rows, part):
        value = base_ref[rows, :] - ratio_ref[rows, :] * part
        x_ref[rows, :] = value
        if m < TILE_ROWS - 1:
            send(m, rows, value, sent_ref, head_ref, rest_ref)

    head_products(kept_ref, far_ref, emit)


def sweep_rest_kernel(
    kept_ref, far_ref, ratio_ref, x_in, sent_in, head_in, x_ref, sent_ref, head_ref
):
    rows, part = rest_product(kept_ref, far_ref)
    value = x_in[rows, :] - ratio_ref[rows, :] * part
    x_ref[rows, :] = value
    send(TILE_ROWS - 1, rows, value, sent_ref, head_ref, None)


def last_head_kernel(kept_ref, far_ref, base_ref, ratio_ref, x_ref):
    def emit(m, rows, part):
        x_ref[rows, :] = base_ref[rows, :] - ratio_ref[rows, :] * part

    head_products(kept_ref, far_ref, emit)


def last_rest_kernel(kept_ref, far_ref, ratio_ref, x_in, x_ref, x_s, sems):
    upper = core_of() == 1
    copies = []
    for m in range(TILE_ROWS - 1):
        done = rows_of(group_of(upper, m))
        copies.append(pltpu.make_async_copy(x_in.at[done, :], x_ref.at[done, :], sems.at[m]))
        copies[m].start()
    rows, part = rest_product(kept_ref, far_ref)
    x_s[...] = x_in[rows, :] - ratio_ref[rows, :] * part
    copies.append(pltpu.make_async_copy(x_s, x_ref.at[rows, :], sems.at[TILE_ROWS - 1]))
    copies[-1].start()
    for copy in copies:
        copy.wait()


def residual_near_kernel(
    straight, kept_ref, own_ref, near_ref, x_ref, right_ref, diag_ref, base_ref
):
    def first(rows, part):
        base_ref[rows, :] = right_ref[rows, :] - diag_ref[rows, :] * x_ref[rows, :] - part

    def second(rows, part):
        base_ref[rows, :] -= part

    near_products(kept_ref, own_ref, near_ref, first, second, straight)


def residual_head_kernel(kept_ref, group_ref, far_ref, base_ref, res_ref, side_ref):
    side_ref[...] = jnp.zeros((QROWS, B), f32)
    upper = core_of() == 1

    def emit(m, rows, part):
        value = base_ref[rows, :] - part
        res_ref[rows, :] = value
        if m < TILE_ROWS - 1:
            for a in range(GROUP):
                group = lax.div(group_ref[group_of(upper, m) * GROUP + a], lax.axis_size("rows"))
                side_ref[pl.ds(pl.multiple_of(group * B, B), B), :] += value[a * B : (a + 1) * B, :]

    head_products(kept_ref, far_ref, emit)


def residual_far_kernel(
    kept_ref, group_ref, far_ref, base_ref, scale_ref, res_ref, side_ref, sent_ref
):
    upper = core_of() == 1
    side_ref[...] = jnp.zeros((QROWS, B), f32)

    def emit(m, rows, part):
        value = base_ref[rows, :] - part
        res_ref[rows, :] = value
        for a in range(GROUP):
            group = lax.div(group_ref[group_of(upper, m) * GROUP + a], lax.axis_size("rows"))
            side_ref[pl.ds(pl.multiple_of(group * B, B), B), :] += value[a * B : (a + 1) * B, :]

    far_products(kept_ref, far_ref, emit)
    value = scale_ref[...] * side_ref[...]
    side_ref[...] = value
    sent_ref[...] = value.astype(bf16)


def residual_rest_kernel(
    kept_ref, tail_ref, far_ref, scale_ref, res_in, side_in, res_ref, side_ref, sent_ref
):
    upper = (core_of() == 1).astype(f32)
    tail = tail_ref[pl.ds(FIELD, TAIL), :].astype(f32)
    rows, part = rest_product(kept_ref, far_ref)
    value = res_in[rows, :] - part
    res_ref[rows, :] = value
    for q in range(4):
        place = pl.ds(q * B, B)
        total = side_in[place, :]
        for a in range(GROUP):
            at = TAIL - GROUP + a
            group = upper * tail[at : at + 1, :] + (1.0 - upper) * tail[a : a + 1, :]
            total = total + jnp.where(group == q, 1.0, 0.0) * value[a * B : (a + 1) * B, :]
        total = scale_ref[place, :] * total
        side_ref[place, :] = total
        sent_ref[place, :] = total.astype(bf16)


def spread(coarse_ref, tail_ref, start, out_ref):
    tail = tail_ref[pl.ds(start, TAIL), :].astype(f32)
    parts = [coarse_ref[pl.ds(q * B, B), :].astype(f32) for q in range(4)]
    for r in range(ROWS):
        group = tail[r : r + 1, :]
        value = jnp.where(group < 0.5, parts[0], parts[1])
        value = jnp.where(group < 1.5, value, parts[2])
        value = jnp.where(group < 2.5, value, parts[3])
        out_ref[pl.ds(r * B, B), :] = value.astype(bf16)


def lift_near_kernel(
    kept_ref, group_ref, coarse_ref, near_ref, near_tail_ref, x_ref, res_ref, ratio_ref, base_ref, own_s, near_s
):
    for r in range(ROWS):
        rows = pl.ds(pl.multiple_of(lax.div(group_ref[r], lax.axis_size("rows")) * B, B), B)
        own_s[pl.ds(r * B, B), :] = coarse_ref[rows, :]
    spread(near_ref, near_tail_ref, FIELD, near_s)

    def first(rows, part):
        base_ref[rows, :] = (
            x_ref[rows, :]
            + (1.0 - RELAX) * own_s[rows, :].astype(f32)
            + ratio_ref[rows, :] * (res_ref[rows, :] - part)
        )

    def second(rows, part):
        base_ref[rows, :] -= ratio_ref[rows, :] * part

    near_products(kept_ref, own_s, near_s, first, second)


def lift_far_kernel(
    kept_ref, far_ref, far_tail_ref, base_ref, ratio_ref, x_ref, sent_ref, head_ref, rest_ref, far_s
):
    spread(far_ref, far_tail_ref, FIELD, far_s)

    def emit(m, rows, part):
        value = base_ref[rows, :] - ratio_ref[rows, :] * part
        x_ref[rows, :] = value
        send(m, rows, value, sent_ref, head_ref, rest_ref)

    far_products(kept_ref, far_s, emit)


def coarse_terms(ops_ref, own_ref, near_ref, far_ref, emit):
    i = lax.axis_index("rows")
    last = lax.axis_size("rows") - 1
    near_is_upper = (core_of() == 0).astype(f32)
    step_up = (i == last).astype(jnp.int32)
    step_down = (i == 0).astype(jnp.int32)
    for q in range(4):
        at_up = pl.multiple_of(jnp.minimum(q + step_up, 3) * B, B)
        at_down = pl.multiple_of(jnp.maximum(q - step_down, 0) * B, B)
        keep_up = (q + step_up <= 3).astype(f32)
        keep_down = (q - step_down >= 0).astype(f32)
        upper = near_is_upper * near_ref[pl.ds(at_up, B), :].astype(f32) + (
            1.0 - near_is_upper
        ) * far_ref[pl.ds(at_up, B), :].astype(f32)
        lower = near_is_upper * far_ref[pl.ds(at_down, B), :].astype(f32) + (
            1.0 - near_is_upper
        ) * near_ref[pl.ds(at_down, B), :].astype(f32)
        field = jnp.concatenate(
            [
                (keep_down * lower).astype(bf16),
                own_ref[pl.ds(q * B, B), :],
                (keep_up * upper).astype(bf16),
            ],
            axis=0,
        )
        ops = jnp.concatenate([ops_ref[q * 3 + d] for d in range(3)], axis=1)
        emit(pl.ds(q * B, B), jnp.dot(ops, field, preferred_element_type=f32))


def ratios():
    sigma = THETA / DELTA
    old = 1.0 / sigma
    out = []
    for _ in range(CHEB - 1):
        new = 1.0 / (2.0 * sigma - old)
        out.append((new * old, 2.0 * new / DELTA))
        old = new
    return out


def coarse_first_kernel(
    ops_ref, side_ref, own_ref, near_ref, far_ref, fix_ref, sent_ref, ops_out_ref
):
    keep, gain = ratios()[0]

    def emit(rows, part):
        side = side_ref[rows, :] / THETA
        fix = side + keep * side + gain * (side_ref[rows, :] - side - part)
        fix_ref[rows, :] = fix
        sent_ref[rows, :] = fix.astype(bf16)

    coarse_terms(ops_ref, own_ref, near_ref, far_ref, emit)
    for n in range(12):
        ops_out_ref[pl.ds(n * B, B), :] = ops_ref[n]


def coarse_second_kernel(ops_ref, side_ref, fix_ref, own_ref, near_ref, far_ref, sent_ref):
    keep, gain = ratios()[1]

    def emit(rows, part):
        fix = fix_ref[rows, :]
        update = fix - side_ref[rows, :] / THETA
        fix = fix + keep * update + gain * (side_ref[rows, :] - fix - part)
        sent_ref[rows, :] = fix.astype(bf16)

    coarse_terms(ops_ref, own_ref, near_ref, far_ref, emit)


def join_kernel(own_ref, near_ref, out_ref):
    out_ref[pl.ds(0, QROWS), :] = own_ref[...]
    out_ref[pl.ds(QROWS, QROWS), :] = near_ref[...]


def coarse_wide_kernel(
    ops_ref, near_ops_ref, far_ops_ref, side_ref, own_ref, near_ref, far_ref, beyond_ref, sent_ref,
    near_s, far_s, fix_s,
):
    i = lax.axis_index("rows")
    last = lax.axis_size("rows") - 1
    near_dir = jnp.where(core_of() == 0, 2, 0)
    far_dir = 2 - near_dir
    far_step = (i == last).astype(jnp.int32) - (i == 0).astype(jnp.int32)
    beyond_step = (i == last - 1).astype(jnp.int32) - (i == 1).astype(jnp.int32)
    keep, gain = ratios()[0]
    keep_next, gain_next = ratios()[1]

    def at(q, step):
        return jnp.clip(q + step, 0, 3)

    def inside(q, step):
        return jnp.logical_and(q + step >= 0, q + step <= 3).astype(f32)

    def block(ref, q, step=None, start=0):
        if step is None:
            return ref[pl.ds(start + q * B, B), :]
        value = ref[pl.ds(pl.multiple_of(start + at(q, step) * B, B), B), :]
        return (inside(q, step) * value.astype(f32)).astype(bf16)

    def product(ops, fields):
        return jnp.dot(
            jnp.concatenate(ops, axis=1),
            jnp.concatenate(fields, axis=0),
            preferred_element_type=f32,
        )

    for q in range(4):
        rows = pl.ds(q * B, B)
        own, near, far = block(own_ref, q), block(near_ref, q), block(far_ref, q, far_step)
        part = product(
            [ops_ref[q * 3 + far_dir], ops_ref[q * 3 + 1], ops_ref[q * 3 + near_dir]],
            [far, own, near],
        )
        side = side_ref[rows, :] / THETA
        fix_s[rows, :] = side + keep * side + gain * (side_ref[rows, :] - side - part)
        ops = [near_ops_ref[pl.ds((q * 3 + d) * B, B), :] for d in range(3)]
        lower_is_own = (near_dir == 2).astype(f32)
        beyond = block(beyond_ref, q, beyond_step).astype(f32)
        own_f = own.astype(f32)
        low = (lower_is_own * own_f + (1.0 - lower_is_own) * beyond).astype(bf16)
        high = (lower_is_own * beyond + (1.0 - lower_is_own) * own_f).astype(bf16)
        part = product(ops, [low, near, high])
        value = near.astype(f32)
        side = value / THETA
        near_s[rows, :] = (side + keep * side + gain * (value - side - part)).astype(bf16)
        first = pl.multiple_of(at(q, far_step) * 3 * B, B)
        ops = [far_ops_ref[pl.ds(pl.multiple_of(first + d * B, B), B), :] for d in range(3)]
        outer = block(far_ref, q, far_step, QROWS).astype(f32)
        low = (lower_is_own * outer + (1.0 - lower_is_own) * own_f).astype(bf16)
        high = (lower_is_own * own_f + (1.0 - lower_is_own) * outer).astype(bf16)
        part = product(ops, [low, far, high])
        value = far.astype(f32)
        side = value / THETA
        fix = side + keep * side + gain * (value - side - part)
        far_s[rows, :] = (inside(q, far_step) * fix).astype(bf16)
    for q in range(4):
        rows = pl.ds(q * B, B)
        fix = fix_s[rows, :]
        part = product(
            [ops_ref[q * 3 + far_dir], ops_ref[q * 3 + 1], ops_ref[q * 3 + near_dir]],
            [far_s[rows, :], fix.astype(bf16), near_s[rows, :]],
        )
        update = fix - side_ref[rows, :] / THETA
        fix = fix + keep_next * update + gain_next * (side_ref[rows, :] - fix - part)
        sent_ref[rows, :] = fix.astype(bf16)


def run(kernel, outs, args, scratch=(), cost=(0, 0), hbm_outs=(), alias={}):
    specs, values = [], []
    for value, space in args:
        if space == "v":
            specs.append(VMEM_SPEC)
            values.append(resident(value))
        elif space == "b":
            specs.append(VMEM_SPEC)
            values.append(value)
        elif space == "s":
            specs.append(SMEM_SPEC)
            values.append(value)
        elif space == "a":
            specs.append(ANY_SPEC)
            values.append(value)
        else:
            specs.append(ANY_SPEC)
            values.append(pltpu.with_memory_space_constraint(value, pltpu.HBM))
    return pl.pallas_call(
        kernel,
        out_shape=[
            jax.ShapeDtypeStruct(shape, dtype) if n in hbm_outs else pltpu.VMEM(shape, dtype)
            for n, (shape, dtype) in enumerate(outs)
        ],
        in_specs=specs,
        out_specs=[ANY_SPEC if n in hbm_outs else VMEM_SPEC for n in range(len(outs))],
        input_output_aliases=alias,
        scratch_shapes=list(scratch),
        cost_estimate=pl.CostEstimate(flops=cost[0], bytes_accessed=cost[1], transcendentals=0),
        compiler_params=pltpu.CompilerParams(vmem_limit_bytes=LIMIT),
    )(*values)


def swap_near(x, size):
    return lax.ppermute(x, "rows", [(i, i ^ 1) for i in range(size)])


def swap_far(x, size):
    pairs = [(i, (i - 1) % size if i % 2 == 0 else (i + 1) % size) for i in range(size)]
    return lax.ppermute(x, "rows", pairs)


FULL = (FIELD, B)
HEAD = (PIECE, B)
REST = (TILE, B)
SIDE = (QROWS, B)
TILE_FLOPS = 2 * TILE * TILE * B
NEAR_COST = (26 * TILE_FLOPS, 8_000_000)
HEAD_COST = (9 * TILE_FLOPS, 3_000_000)
REST_COST = (TILE_FLOPS, 1_000_000)
FIELDS = [(FULL, f32), (FULL, bf16), (HEAD, bf16), (REST, bf16)]


def shards(right_side, fine_blocks, fine_columns, fine_diag, aggregate, coarse_blocks, coarse_diag):
    size = lax.axis_size("rows")

    first, sent, ratio, diag, packed, places_of = run(
        start_kernel,
        [
            (FULL, f32), ((FIELD + TAIL, B), bf16),
            (FULL, f32), (FULL, f32), ((3 * B + TAIL, B), bf16),
            ((ROWS, B), jnp.int32),
        ],
        [
            (right_side, "h"), (fine_diag.reshape(ROWS, B), "h"), (aggregate, "h"),
            (coarse_blocks, "h"), (coarse_diag.reshape(1, B), "h"),
            (fine_columns, "h"),
        ],
        [
            pltpu.VMEM(FULL, f32),
            pltpu.VMEM((ROWS, B), f32),
            pltpu.SMEM((ROWS,), jnp.int32),
            pltpu.VMEM((1, 3, B, B), f32),
            pltpu.VMEM((1, B), f32),
            pltpu.VMEM((ROWS, 2 * ROWS), jnp.int32),
            pltpu.SemaphoreType.DMA((TILE_ROWS + 5,)),
        ],
    )

    def swap_fields(sent, head, rest):
        return swap_far(head, size), swap_far(rest, size), swap_near(sent, size)

    def swap_sides(sent):
        return swap_far(sent, size), swap_near(sent, size)

    pieces = [packed] + [
        lax.ppermute(packed, "rhs", [(i, (i + k) % 4) for i in range(4)]) for k in range(1, 4)
    ]
    far, near = swap_sides(sent)
    own_tail, near_tail, far_tail = sent, near, far
    kept, base = run(
        load_near_kernel,
        [((ROWS * SLOTS, B, B), bf16), (FULL, f32)],
        [
            (places_of, "s"), (fine_blocks, "h"), (sent, "v"), (near, "v"), (first, "v"),
            (ratio, "v"),
        ],
        [pltpu.SemaphoreType.DMA((TILE_ROWS,))],
        (NEAR_COST[0], 28_000_000),
    )

    def sweep_start(x, sent, near):
        return run(
            sweep_near_kernel,
            [(FULL, f32)],
            [(kept, "v"), (sent, "v"), (near, "v"), (x, "v"), (first, "v"), (ratio, "v")],
            cost=NEAR_COST,
        )[0]

    def sweep_end(far, far_rest, base):
        x, sent, head, rest = run(
            sweep_head_kernel,
            FIELDS,
            [(kept, "v"), (far, "v"), (base, "v"), (ratio, "v")],
            cost=HEAD_COST,
        )
        x, sent, head = run(
            sweep_rest_kernel,
            FIELDS[:3],
            [(kept, "v"), (far_rest, "v"), (ratio, "v"), (x, "v"), (sent, "v"), (head, "v")],
            cost=REST_COST,
            alias={3: 0, 4: 1, 5: 2},
        )
        return x, sent, head, rest

    x = first
    for turn in range(CYCLES):
        for _ in range(2 * (turn > 0)):
            far, far_rest, near = swap_fields(sent, head, rest)
            base = sweep_start(x, sent, near)
            x, sent, head, rest = sweep_end(far, far_rest, base)
        if turn == 0:
            x, sent = run(
                sweep_far_kernel,
                FIELDS[:2],
                [(kept, "v"), (far, "v"), (base, "v"), (ratio, "v")],
                cost=HEAD_COST,
            )
        if turn == 0:
            far, near = swap_sides(sent)
        else:
            far, far_rest, near = swap_fields(sent, head, rest)
        (base,) = run(
            functools.partial(residual_near_kernel, turn == 0),
            [(FULL, f32)],
            [(kept, "v"), (sent, "v"), (near, "v"), (x, "v"), (right_side, "b"), (diag, "v")],
            cost=NEAR_COST,
        )
        if turn == 0:
            ops, scale = run(
                sort_kernel,
                [((12, B, B), bf16), (SIDE, f32)],
                [(p, "v") for p in pieces] + [(base, "v")],
            )
            res, side, sent = run(
                residual_far_kernel,
                [(FULL, f32), (SIDE, f32), (SIDE, bf16)],
                [(kept, "v"), (aggregate, "s"), (far, "v"), (base, "v"), (scale, "v")],
                cost=HEAD_COST,
            )
        else:
            res, side = run(
                residual_head_kernel,
                [(FULL, f32), (SIDE, f32)],
                [(kept, "v"), (aggregate, "s"), (far, "v"), (base, "v")],
                cost=HEAD_COST,
            )
            res, side, sent = run(
                residual_rest_kernel,
                [(FULL, f32), (SIDE, f32), (SIDE, bf16)],
                [
                    (kept, "v"), (own_tail, "v"), (far_rest, "v"), (scale, "v"), (res, "v"),
                    (side, "v"),
                ],
                cost=REST_COST,
                alias={4: 0, 5: 1},
            )
        if turn == 0:
            far, near = swap_sides(sent)
            fix, sent, ops_sent = run(
                coarse_first_kernel,
                [(SIDE, f32), (SIDE, bf16), ((12 * B, B), bf16)],
                [(ops, "v"), (side, "v"), (sent, "v"), (near, "v"), (far, "v")],
            )
            far, near = swap_sides(sent)
            far_ops, near_ops = swap_sides(ops_sent)
            (sent,) = run(
                coarse_second_kernel,
                [(SIDE, bf16)],
                [(ops, "v"), (side, "v"), (fix, "v"), (sent, "v"), (near, "v"), (far, "v")],
            )
        else:
            near = swap_near(sent, size)
            (pair,) = run(join_kernel, [((2 * QROWS, B), bf16)], [(sent, "v"), (near, "v")])
            far = swap_far(pair, size)
            beyond = swap_near(far, size)
            (sent,) = run(
                coarse_wide_kernel,
                [(SIDE, bf16)],
                [
                    (ops, "v"), (near_ops, "v"), (far_ops, "v"), (side, "v"), (sent, "v"),
                    (near, "v"), (far, "v"), (beyond, "v"),
                ],
                [pltpu.VMEM(SIDE, bf16), pltpu.VMEM(SIDE, bf16), pltpu.VMEM(SIDE, f32)],
            )
        far, near = swap_sides(sent)
        (base,) = run(
            lift_near_kernel,
            [(FULL, f32)],
            [
                (kept, "v"), (aggregate, "s"), (sent, "v"), (near, "v"), (near_tail, "v"),
                (x, "v"), (res, "v"), (ratio, "v"),
            ],
            [pltpu.VMEM(FULL, bf16), pltpu.VMEM(FULL, bf16)],
            NEAR_COST,
        )
        x, sent, head, rest = run(
            lift_far_kernel,
            FIELDS,
            [(kept, "v"), (far, "v"), (far_tail, "v"), (base, "v"), (ratio, "v")],
            [pltpu.VMEM(FULL, bf16)],
            (10 * TILE_FLOPS, 3_000_000),
        )
        far, far_rest, near = swap_fields(sent, head, rest)
        base = sweep_start(x, sent, near)
        if turn < CYCLES - 1:
            x, sent, head, rest = sweep_end(far, far_rest, base)
    (x,) = run(
        last_head_kernel,
        [(FULL, f32)],
        [(kept, "v"), (far, "v"), (base, "v"), (ratio, "v")],
        cost=HEAD_COST,
    )
    (x,) = run(
        last_rest_kernel,
        [(FULL, f32)],
        [(kept, "v"), (far_rest, "v"), (ratio, "v"), (x, "v")],
        [pltpu.VMEM(REST, f32), pltpu.SemaphoreType.DMA((TILE_ROWS,))],
        REST_COST,
        hbm_outs=(0,),
    )
    return x


def solution(mesh):
    in_specs = (
        P("rows", "rhs"),
        P("rows", None, None, None),
        P("rows", None),
        P("rows"),
        P("rows"),
        P(("rhs", "rows"), None, None, None),
        P(("rhs", "rows")),
    )
    return jax.shard_map(
        shards, mesh=mesh, in_specs=in_specs, out_specs=P("rows", "rhs"), check_vma=False
    )
```
